32 devices in a mesh: sky: 4 (over z), chan: 8 (over y, x, core).
Axes of the slice: x: 2, y: 2, z: 4, core: 2. Of those that a mesh axis runs over, the one named last changes fastest.
Arguments:
- beam_images: float32 [16, 2, 288, 16384], P('sky', None, 'chan'), may hold values from -6 to 6
- beam_weights: float32 [16, 16384], P('sky'), may hold values from 0.05 to 1
- offsets: int32 [16], P('sky'), may hold values from 0 to 65535, as said below
Outputs:
- beam_residuals: float32 [16, 2, 288, 16384], P('sky', None, 'chan')
- depth_model: float32 [2, 512, 65536], P(None, None, ('sky', 'chan'))
The draws below stay inside these ranges and needn't reach their ends.
Inputs may be any that keep to these rules, and one draw needn't show every extreme that they name: `offsets`: beam b starts in tile b // 4: its offset lies in [(b // 4) * 16384, (b // 4 + 1) * 16384).
All inputs are finite; a program needn't handle non-finite values.
Results may differ from the reference program's by a relative error of at most 0.00045.
Values sent between devices are 32-bit elements; how exact they have to be, the bound alone decides.
No kernel may reach another device: no remote copies, remote signals or barrier semaphores. Data moves between devices by JAX's collectives and lax.ppermute only.
A program may use at most 128 MiB of HBM per device.

```python
import math
import jax
import jax.numpy as jnp
from jax import lax

C = 288
F = 512
PIX_SKY = 16384
BEAMS_DEV = 4
ITERS = 3
BEAMS = 16
NPIX = 65536


def draw_offsets(key, part):
    tiles = jnp.arange(BEAMS, dtype=jnp.int32) // BEAMS_DEV * PIX_SKY
    return tiles + jax.random.randint(jax.random.fold_in(key, 17), (BEAMS,), 0, PIX_SKY, dtype=jnp.int32)


def level_of(key, shape, pieces, low, largest):
    level, own = 1.0, jax.random.fold_in(key, 6)
    for position, parts in pieces:
        draws = jnp.exp(jax.random.uniform(jax.random.fold_in(own, position), (parts,), jnp.float32, low / len(pieces), largest / len(pieces)))
        level = level * jnp.repeat(draws, shape[position] // parts).reshape([-1 if axis == position else 1 for axis in range(len(shape))])
    return level


def gaussian(own_key, extent, width, bound, pieces=(), kind=jnp.bfloat16):
    factor_of = level_of(own_key, extent, pieces, -0.22, 0.18) if pieces else 1.0
    array = jax.random.normal(own_key, extent, jnp.float32) * width * factor_of
    return jnp.minimum(jnp.maximum(array, -bound), bound).astype(kind)


def setup_inputs(seed: int = 0) -> dict:
    arg_keys = jax.random.split(jax.random.key(seed), 4)
    beam_images = gaussian(arg_keys[0], (BEAMS, 2, C, PIX_SKY), 1.0, 6.0, ((0, 4), (2, 8)), jnp.float32)
    beam_weights = jnp.clip(jnp.exp(math.log(1.0) - 2.9957323 * jax.random.uniform(arg_keys[1], (BEAMS, PIX_SKY), jnp.float32) ** level_of(arg_keys[1], (BEAMS, PIX_SKY), ((0, 4),), -0.2, 0.2)), 0.05, 1.0)
    offsets = draw_offsets(jax.random.fold_in(arg_keys[3], 71), 0)
    return {"beam_images": beam_images, "beam_weights": beam_weights, "offsets": offsets}


BAND_LOW = 800000000.0
BAND_WIDTH = 288000000.0
LIGHT = 299792458.0
DEPTH_STEP = 20.0
COMBINE_FLOOR = 0.5
THRESH_FRAC = 0.25
THRESH_BASE = 0.005
STEP_GAIN = 0.5

def depth_tables():
    channel = jnp.arange(C, dtype=jnp.float32)
    freq = BAND_LOW + (channel + 0.5) * (BAND_WIDTH / C)
    lam_sq = (LIGHT / freq) ** 2
    lam_sq = lam_sq - jnp.mean(lam_sq)
    depth = (jnp.arange(F, dtype=jnp.float32) - F // 2) * DEPTH_STEP
    angle = 2.0 * depth[:, None] * lam_sq[None, :]
    cosine = jnp.cos(angle)
    sine = jnp.sin(angle)
    synth = jnp.concatenate([jnp.concatenate([cosine, sine], 1), jnp.concatenate([-sine, cosine], 1)], 0) / C
    forward = jnp.concatenate([jnp.concatenate([cosine.T, -sine.T], 1), jnp.concatenate([sine.T, cosine.T], 1)], 0)
    return (synth, forward)

def matmul(left, right):
    return jnp.dot(left, right, preferred_element_type=jnp.float32, precision=lax.Precision.HIGHEST)

def magnitude(field):
    return jnp.sqrt(field[:F] ** 2 + field[F:] ** 2)

def shrink(field, thresh):
    mag = magnitude(field)
    factor = jnp.maximum(mag - thresh, 0.0) / jnp.maximum(mag, thresh)
    return field * jnp.concatenate([factor, factor], 0)

def deconvolve(combined, synth, forward):
    dirty = matmul(synth, combined)
    thresh = THRESH_FRAC * lax.optimization_barrier(jnp.max(magnitude(dirty), axis=0, keepdims=True)) + THRESH_BASE
    model = jnp.zeros(dirty.shape, jnp.float32)
    for step in range(ITERS):
        resid = combined - matmul(forward, model)
        model = shrink(model + STEP_GAIN * matmul(synth, resid), thresh)
    resid = combined - matmul(forward, model)
    return (model, resid)

def reference(beam_images, beam_weights, offsets):
    total = NPIX + PIX_SKY
    numer = jnp.zeros((2, C, total), jnp.float32)
    wsum = jnp.zeros((total,), jnp.float32)

    def add_beam(index, carry):
        numer, wsum = carry
        start = offsets[index].astype(jnp.int32)
        weight = beam_weights[index]
        old = lax.dynamic_slice_in_dim(numer, start, PIX_SKY, 2)
        numer = lax.dynamic_update_slice_in_dim(numer, old + weight * beam_images[index], start, 2)
        oldw = lax.dynamic_slice_in_dim(wsum, start, PIX_SKY, 0)
        wsum = lax.dynamic_update_slice_in_dim(wsum, oldw + weight, start, 0)
        return (numer, wsum)
    numer, wsum = lax.fori_loop(0, BEAMS, add_beam, (numer, wsum))
    combined = numer[:, :, :NPIX] / (wsum[:NPIX] + COMBINE_FLOOR)
    synth, forward = depth_tables()
    model, resid = deconvolve(combined.reshape(2 * C, NPIX), synth, forward)
    padded = jnp.concatenate([resid.reshape(2, C, NPIX), jnp.zeros((2, C, PIX_SKY), jnp.float32)], 2)

    def read_beam(pair):
        weight, start = pair
        return weight * lax.dynamic_slice_in_dim(padded, start.astype(jnp.int32), PIX_SKY, 2)
    beam_residuals = lax.map(read_beam, (beam_weights, offsets))
    return (beam_residuals, model.reshape(2, F, NPIX))
```

```python
import functools

import jax
import jax.numpy as jnp
from jax import lax
from jax.experimental import pallas as pl
from jax.experimental.pallas import tpu as pltpu
from jax.sharding import PartitionSpec as P

ITERS = 3

BAND_LOW = 800000000.0
BAND_WIDTH = 288000000.0
LIGHT = 299792458.0
DEPTH_STEP = 20.0
COMBINE_FLOOR = 0.5
THRESH_FRAC = 0.25
THRESH_BASE = 0.005
STEP_GAIN = 0.5

LANES = 128
CHUNK = 512
VMEM = 60 * 1024 * 1024


def split_rows(arrays):
    high = lax.reduce_precision(arrays, 8, 7)
    return high.astype(jnp.bfloat16), (arrays - high).astype(jnp.bfloat16)


def depth_tables(channels, depths):
    half = depths // 2
    channel = jnp.arange(channels, dtype=jnp.float32)
    freq = BAND_LOW + (channel + 0.5) * (BAND_WIDTH / channels)
    lam_sq = (LIGHT / freq) ** 2
    lam_sq = lam_sq - jnp.mean(lam_sq)
    depth = (jnp.arange(half, dtype=jnp.float32) + 1.0) * DEPTH_STEP
    angle = 2.0 * depth[:, None] * lam_sq[None, :]
    cosine = jnp.cos(angle)
    sine = jnp.sin(angle)
    ones = jnp.concatenate([jnp.ones((1, channels)), jnp.zeros((15, channels))], 0)
    synth = jnp.concatenate([cosine, sine, ones], 0) / channels * STEP_GAIN
    high, low = split_rows(synth)
    pad = -3 * channels % LANES
    synth = jnp.concatenate([high, high, low, jnp.zeros((high.shape[0], pad), jnp.bfloat16)], 1)
    forward = jnp.concatenate([cosine, sine], 0).T
    high, low = split_rows(forward)
    return synth, jnp.concatenate([high, high, low], 1)


def place(offsets_ref, beam, axis):
    start = offsets_ref[beam]
    return lax.div(start, LANES), lax.rem(start, LANES)


def gather_kernel(half, chunks, offsets_ref, weights_ref, images_ref, *rest):
    outs, wsum_ref, shifted = rest[:chunks], rest[chunks], rest[chunks + 1]
    beams, block, rows, _ = images_ref.shape
    step = 64
    lane = lax.broadcasted_iota(jnp.int32, (step, LANES), 1)
    places = [place(offsets_ref, beam, None) for beam in range(beams)]

    @pl.when(pl.program_id(0) == 0)
    def _():
        margin = jnp.zeros((rows, LANES), jnp.float32)
        for slot in range(2):
            for beam in range(beams):
                shifted[slot, beam, :rows, :] = margin
                shifted[slot, beam, 2 * rows :, :] = margin

    def emit(slot, value_of, store):
        for beam in range(beams):
            for row in range(0, rows, step):
                shifted[slot, beam, rows + row : rows + row + step, :] = pltpu.roll(
                    value_of(beam, row), places[beam][1], 1
                )
        for row in range(0, rows, step):
            total = None
            for beam in range(beams):
                tile, rest_px = places[beam]
                base = (half + 1) * rows + row - 2 * tile
                here = shifted[slot, beam, pl.ds(base, step), :]
                before = shifted[slot, beam, pl.ds(base - 2, step), :]
                part = jnp.where(lane >= rest_px, here, before)
                total = part if total is None else total + part
            store(row, total)

    @pl.when(pl.program_id(0) == 0)
    def _():
        def store(row, total):
            wsum_ref[row : row + step, :] = total

        emit(1, lambda beam, row: weights_ref[beam, row : row + step, :], store)

    for channel in range(block):

        def store(row, total):
            rows_out = outs[0].shape[2]
            for piece in range(step // rows_out):
                where = row // rows_out + piece
                outs[where % chunks][where // chunks, channel] = total[
                    piece * rows_out : (piece + 1) * rows_out
                ]

        emit(
            channel % 2,
            lambda beam, row: images_ref[beam, channel, row : row + step, :]
            * weights_ref[beam, row : row + step, :],
            store,
        )


def channel_block(channels):
    return max(size for size in range(1, 5) if channels % size == 0)


def gather(half, members, chunks, starts, weights, images):
    beams, channels, rows, _ = images.shape
    block = channel_block(channels)
    rows_out = rows // (members * chunks)
    piece = jax.ShapeDtypeStruct((members, channels, rows_out, LANES), jnp.float32)
    result = pl.pallas_call(
        functools.partial(gather_kernel, half, chunks),
        grid_spec=pltpu.PrefetchScalarGridSpec(
            num_scalar_prefetch=1,
            grid=(channels // block,),
            in_specs=[
                pl.BlockSpec((beams, rows, LANES), lambda step, _: (0, 0, 0)),
                pl.BlockSpec((beams, block, rows, LANES), lambda step, _: (0, step, 0, 0)),
            ],
            out_specs=[
                pl.BlockSpec((members, block, rows_out, LANES), lambda step, _: (0, step, 0, 0))
            ]
            * chunks
            + [pl.BlockSpec((rows, LANES), lambda step, _: (0, 0))],
            scratch_shapes=[pltpu.VMEM((2, beams, 3 * rows, LANES), jnp.float32)],
        ),
        out_shape=[piece] * chunks + [jax.ShapeDtypeStruct((rows, LANES), jnp.float32)],
        compiler_params=pltpu.CompilerParams(vmem_limit_bytes=VMEM),
        name="gather_own" if half == 0 else "gather_next",
    )(starts, weights, images)
    return result[:chunks], result[chunks]


def scatter_kernel(chunks, offsets_ref, weights_ref, *rest):
    own, following = rest[:chunks], rest[chunks : 2 * chunks]
    out_ref, joined = rest[2 * chunks :]
    beams, block, rows, _ = out_ref.shape
    members, rows_in = own[0].shape[0], own[0].shape[2]
    step = 64
    lane = lax.broadcasted_iota(jnp.int32, (step, LANES), 1)
    places = [place(offsets_ref, beam, None) for beam in range(beams)]
    for channel in range(block):
        slot = channel % 2
        for half, pieces in enumerate((own, following)):
            for member in range(members):
                for chunk in range(chunks):
                    row = half * rows + (member * chunks + chunk) * rows_in
                    joined[slot, row : row + rows_in, :] = pieces[chunk][member, channel]
        for beam in range(beams):
            tile, rest_px = places[beam]
            for row in range(0, rows, step):
                base = 2 * tile + row
                here = joined[slot, pl.ds(base, step), :]
                after = joined[slot, pl.ds(base + 2, step), :]
                value = jnp.where(lane >= rest_px, here, after)
                value = pltpu.roll(value, lax.rem(LANES - rest_px, LANES), 1)
                out_ref[beam, channel, row : row + step, :] = (
                    value * weights_ref[beam, row : row + step, :]
                )


def scatter(starts, weights, own, following):
    chunks = len(own)
    beams, rows, _ = weights.shape
    members, channels, rows_in, _ = own[0].shape
    block = channel_block(channels)
    return pl.pallas_call(
        functools.partial(scatter_kernel, chunks),
        grid_spec=pltpu.PrefetchScalarGridSpec(
            num_scalar_prefetch=1,
            grid=(channels // block,),
            in_specs=[pl.BlockSpec((beams, rows, LANES), lambda step, _: (0, 0, 0))]
            + [pl.BlockSpec((members, block, rows_in, LANES), lambda step, _: (0, step, 0, 0))]
            * (2 * chunks),
            out_specs=pl.BlockSpec((beams, block, rows, LANES), lambda step, _: (0, step, 0, 0)),
            scratch_shapes=[pltpu.VMEM((2, 2 * rows, LANES), jnp.float32)],
        ),
        out_shape=jax.ShapeDtypeStruct((beams, channels, rows, LANES), jnp.float32),
        compiler_params=pltpu.CompilerParams(vmem_limit_bytes=VMEM),
        name="scatter",
    )(starts, weights, *own, *following)


def split(value):
    high = value.astype(jnp.bfloat16)
    return high, (value - high.astype(jnp.float32)).astype(jnp.bfloat16)


def deconvolve_kernel(aliased, *refs):
    if aliased:
        refs = refs[:3] + refs[4:]
    flat_ref, synth_ref, forward_ref, resid_ref, model_ref = refs[:5]
    flat, resid, x, y, product, field, power, limit = refs[5:]
    channels, pixels = flat.shape[0], flat.shape[1] // 2
    half = field.shape[1]
    tiles = pixels // LANES
    stride = 2 * tiles
    sub = 16
    views = ((0, slice(0, pixels)), (1, slice(pixels, 2 * pixels)))

    for q in range(2):
        for tile in range(tiles):
            lanes = slice(q * pixels + tile * LANES, q * pixels + (tile + 1) * LANES)
            flat[:, lanes] = flat_ref[pl.ds(2 * tile + q, channels, stride=stride), :]
    x[3 * channels :, :] = jnp.zeros((x.shape[0] - 3 * channels, 2 * pixels), jnp.bfloat16)

    def feed(row, value):
        high, low = split(value)
        rows = value.shape[0]
        x[pl.ds(row, rows), :] = high
        x[pl.ds(channels + row, rows), :] = low
        x[pl.ds(2 * channels + row, rows), :] = high

    def first(index, carry):
        row = pl.multiple_of(index * sub, sub)
        feed(row, flat[pl.ds(row, sub), :])
        return carry

    lax.fori_loop(0, channels // sub, first, 0)
    zero = jnp.zeros((sub, pixels), jnp.float32)

    def clear(index, carry):
        row = pl.multiple_of(index * sub, sub)
        for part in range(4):
            field[part, pl.ds(row, sub), :] = zero
        return carry

    lax.fori_loop(0, half // sub, clear, 0)

    def last_row(row):
        return lax.broadcasted_iota(jnp.int32, (sub, pixels), 0) + row == half - 1

    def iterate(number, carry):
        product[...] = jnp.dot(synth_ref[...], x[...], preferred_element_type=jnp.float32)
        middle_q = product[2 * half : 2 * half + 1, :pixels]
        middle_u = product[2 * half : 2 * half + 1, pixels:]

        def advance(index, largest):
            row = pl.multiple_of(index * sub, sub)
            cos_q = product[pl.ds(row, sub), :pixels]
            cos_u = product[pl.ds(row, sub), pixels:]
            sin_q = product[pl.ds(half + row, sub), :pixels]
            sin_u = product[pl.ds(half + row, sub), pixels:]
            last = last_row(row)
            real_p = field[0, pl.ds(row, sub), :] + jnp.where(last, middle_q, cos_q + sin_u)
            real_n = field[1, pl.ds(row, sub), :] + (cos_q - sin_u)
            imag_p = field[2, pl.ds(row, sub), :] + jnp.where(last, middle_u, cos_u - sin_q)
            imag_n = field[3, pl.ds(row, sub), :] + (cos_u + sin_q)
            power_p = real_p * real_p + imag_p * imag_p
            power_n = real_n * real_n + imag_n * imag_n
            field[0, pl.ds(row, sub), :] = real_p
            field[1, pl.ds(row, sub), :] = real_n
            field[2, pl.ds(row, sub), :] = imag_p
            field[3, pl.ds(row, sub), :] = imag_n
            power[0, pl.ds(row, sub), :] = power_p
            power[1, pl.ds(row, sub), :] = power_n
            return jnp.maximum(largest, jnp.maximum(power_p, power_n))

        largest = lax.fori_loop(0, half // sub, advance, zero)

        @pl.when(number == 0)
        def _():
            top = jnp.sqrt(jnp.max(largest, axis=0, keepdims=True))
            limit[...] = jnp.broadcast_to(THRESH_FRAC / STEP_GAIN * top + THRESH_BASE, limit.shape)

        level = jnp.concatenate([limit[...], limit[...]], 0)

        def shrink(index, carry):
            row = pl.multiple_of(index * sub, sub)
            factor_p = jnp.maximum(1.0 - level * lax.rsqrt(power[0, pl.ds(row, sub), :]), 0.0)
            factor_n = jnp.maximum(1.0 - level * lax.rsqrt(power[1, pl.ds(row, sub), :]), 0.0)
            real_p = field[0, pl.ds(row, sub), :] * factor_p
            real_n = field[1, pl.ds(row, sub), :] * factor_n
            imag_p = field[2, pl.ds(row, sub), :] * factor_p
            imag_n = field[3, pl.ds(row, sub), :] * factor_n
            field[0, pl.ds(row, sub), :] = real_p
            field[1, pl.ds(row, sub), :] = real_n
            field[2, pl.ds(row, sub), :] = imag_p
            field[3, pl.ds(row, sub), :] = imag_n
            last = last_row(row)
            real_p = jnp.where(last, 0.0, real_p)
            imag_p = jnp.where(last, 0.0, imag_p)
            for base, left, right in (
                (0, real_p + real_n, imag_p + imag_n),
                (half, imag_n - imag_p, real_p - real_n),
            ):
                for value, lanes in ((left, slice(0, pixels)), (right, slice(pixels, 2 * pixels))):
                    high, low = split(value)
                    y[pl.ds(base + row, sub), lanes] = high
                    y[pl.ds(2 * half + base + row, sub), lanes] = low
            return carry

        lax.fori_loop(0, half // sub, shrink, 0)
        resid[...] = jnp.dot(
            forward_ref[:, : 4 * half], y[...], preferred_element_type=jnp.float32
        ) + jnp.dot(
            forward_ref[:, 4 * half :], y[: 2 * half, :], preferred_element_type=jnp.float32
        )
        middle = jnp.concatenate(
            [field[0, half - 1 : half, :], field[2, half - 1 : half, :]], 1
        )

        def subtract(index, carry):
            row = pl.multiple_of(index * sub, sub)
            value = flat[pl.ds(row, sub), :] - (resid[pl.ds(row, sub), :] + middle)
            resid[pl.ds(row, sub), :] = value
            feed(row, value)
            return carry

        lax.fori_loop(0, channels // sub, subtract, 0)
        return carry

    lax.fori_loop(0, ITERS, iterate, 0)

    for q in range(2):
        for tile in range(tiles):
            lanes = slice(q * pixels + tile * LANES, q * pixels + (tile + 1) * LANES)
            resid_ref[pl.ds(2 * tile + q, channels, stride=stride), :] = resid[:, lanes]

    for part in range(2):
        model_ref[part, half : half + 1, :] = field[2 * part, half - 1 : half, :]
        model_ref[part, half + 1 :, :] = field[2 * part, : half - 1, :]

    def reverse(index, carry):
        row = pl.multiple_of(index * 8, 8)
        for part in range(2):
            value = field[2 * part + 1, pl.ds(row, 8), :]
            for line in range(8):
                model_ref[part, pl.ds(half - 1 - line - row, 1), :] = value[line : line + 1, :]
        return carry

    lax.fori_loop(0, half // 8, reverse, 0)


def deconvolve(chunk, depths, pixels, cube, synth, forward, model):
    members, group, rows, _ = cube.shape
    channels = members * group
    half = depths // 2
    size = rows // 2 * LANES
    flat = cube.reshape(channels * rows, LANES)
    whole = pl.BlockSpec(flat.shape, lambda step: (0, 0))
    aliased = model is not None
    resid, model = pl.pallas_call(
        functools.partial(deconvolve_kernel, aliased),
        grid=(1,),
        in_specs=[
            whole,
            pl.BlockSpec(synth.shape, lambda step: (0, 0)),
            pl.BlockSpec(forward.shape, lambda step: (0, 0)),
        ]
        + [pl.BlockSpec(memory_space=pl.ANY)] * aliased,
        out_specs=[whole, pl.BlockSpec((2, depths, size), lambda step: (0, 0, chunk))],
        out_shape=[
            jax.ShapeDtypeStruct(flat.shape, jnp.float32),
            jax.ShapeDtypeStruct((2, depths, pixels), jnp.float32),
        ],
        scratch_shapes=[
            pltpu.VMEM((channels, 2 * size), jnp.float32),
            pltpu.VMEM((channels, 2 * size), jnp.float32),
            pltpu.VMEM((synth.shape[1], 2 * size), jnp.bfloat16),
            pltpu.VMEM((4 * half, 2 * size), jnp.bfloat16),
            pltpu.VMEM((synth.shape[0], 2 * size), jnp.float32),
            pltpu.VMEM((4, half, size), jnp.float32),
            pltpu.VMEM((2, half, size), jnp.float32),
            pltpu.VMEM((8, size), jnp.float32),
        ],
        input_output_aliases={3: 1} if aliased else {},
        compiler_params=pltpu.CompilerParams(vmem_limit_bytes=VMEM),
        name="deconvolve",
    )(flat, synth, forward, *([model] if aliased else []))
    return resid.reshape(cube.shape), model


def body(depths, chunk_pixels, beam_images, beam_weights, offsets):
    beams, _, group, tile = beam_images.shape
    members = lax.axis_size("chan")
    sky = lax.axis_size("sky")
    pixels = tile // members
    chunks = max(1, pixels // chunk_pixels)
    lines = tile // LANES
    channels = group * members
    starts = offsets - lax.axis_index("sky") * tile
    images = beam_images.reshape(beams, 2, group, lines, LANES).transpose(0, 2, 3, 1, 4)
    images = images.reshape(beams, group, 2 * lines, LANES)
    weights = jnp.repeat(beam_weights.reshape(beams, lines, LANES), 2, axis=1)
    forward_pairs = [(index, index + 1) for index in range(sky - 1)]
    backward_pairs = [(index + 1, index) for index in range(sky - 1)]

    spill, spill_w = gather(1, members, chunks, starts, weights, images)
    arrived_w = lax.ppermute(spill_w, "sky", forward_pairs)
    arrived = [lax.ppermute(part, "sky", forward_pairs) for part in spill]
    own, own_w = gather(0, members, chunks, starts, weights, images)
    scale = (own_w + arrived_w + COMBINE_FLOOR).reshape(members, 1, chunks, -1, LANES)
    synth, forward = depth_tables(channels, depths)

    model = None
    resid, following = [], []
    for chunk in range(chunks):
        combined = (own[chunk] + arrived[chunk]) / scale[:, :, chunk]
        cube = lax.all_to_all(combined, "chan", 0, 0, tiled=True)
        part, model = deconvolve(chunk, depths, pixels, cube, synth, forward, model)
        part = lax.all_to_all(part, "chan", 0, 0, tiled=True)
        resid.append(part)
        following.append(lax.ppermute(part, "sky", backward_pairs))
    outputs = scatter(starts, weights, resid, following)
    outputs = outputs.reshape(beams, group, lines, 2, LANES).transpose(0, 3, 1, 2, 4)
    return outputs.reshape(beam_images.shape), model


DEPTHS = 512


def solution(mesh):
    in_specs = (P("sky", None, "chan", None), P("sky", None), P("sky"))
    out_specs = (P("sky", None, "chan", None), P(None, None, ("sky", "chan")))
    return jax.shard_map(
        functools.partial(body, DEPTHS, CHUNK),
        mesh=mesh,
        in_specs=in_specs,
        out_specs=out_specs,
        check_vma=False,
    )
```

```python
import functools

import jax
import jax.numpy as jnp
from jax import lax
from jax.experimental import pallas as pl
from jax.experimental.pallas import tpu as pltpu
from jax.sharding import PartitionSpec as P


ITERS = 3

BAND_LOW = 800000000.0
BAND_WIDTH = 288000000.0
LIGHT = 299792458.0
DEPTH_STEP = 20.0
COMBINE_FLOOR = 0.5
THRESH_FRAC = 0.25
THRESH_BASE = 0.005
STEP_GAIN = 0.5

LANES = 128
GROUP = 128
VMEM = 60 * 1024 * 1024


def split_rows(arrays):
    high = lax.reduce_precision(arrays, 8, 7)
    return high.astype(jnp.bfloat16), (arrays - high).astype(jnp.bfloat16)


def depth_tables(channels, depths):
    half = depths // 2
    channel = jnp.arange(channels, dtype=jnp.float32)
    freq = BAND_LOW + (channel + 0.5) * (BAND_WIDTH / channels)
    lam_sq = (LIGHT / freq) ** 2
    lam_sq = lam_sq - jnp.mean(lam_sq)
    depth = (jnp.arange(half, dtype=jnp.float32) + 1.0) * DEPTH_STEP
    angle = 2.0 * depth[:, None] * lam_sq[None, :]
    cosine = jnp.cos(angle)
    sine = jnp.sin(angle)
    ones = jnp.concatenate([jnp.ones((1, channels)), jnp.zeros((15, channels))], 0)
    synth = jnp.concatenate([cosine, sine, ones], 0) / channels * STEP_GAIN
    high, low = split_rows(synth)
    pad = -3 * channels % LANES
    synth = jnp.concatenate([high, high, low, jnp.zeros((high.shape[0], pad), jnp.bfloat16)], 1)
    forward = jnp.concatenate([cosine, sine], 0).T
    high, low = split_rows(forward)
    return synth, jnp.concatenate([high, high, low], 1)


def place(offsets_ref, beam):
    start = offsets_ref[beam]
    return lax.div(start, LANES), lax.rem(start, LANES)


def gather_kernel(spans, offsets_ref, weights_ref, images_ref, *rest):
    chunks = len(spans)
    own, following = rest[:chunks], rest[chunks : 2 * chunks]
    wsum_ref, shifted = rest[2 * chunks], rest[2 * chunks + 1 :]
    beams, block, rows, _ = images_ref.shape
    members = own[0].shape[0]
    share = rows // members
    step = max(64, share)
    lane = lax.broadcasted_iota(jnp.int32, (step, LANES), 1)
    places = [place(offsets_ref, beam) for beam in range(beams)]

    @pl.when(pl.program_id(0) == 0)
    def _():
        margin = jnp.zeros((rows, LANES), jnp.float32)
        for scratch in shifted:
            for beam in range(beams):
                scratch[beam, :rows, :] = margin
                scratch[beam, 2 * rows :, :] = margin

    def shift(scratch, beam, row, value):
        scratch[beam, rows + row : rows + row + step, :] = pltpu.roll(value, places[beam][1], 1)

    def total(scratch, half, row):
        result = None
        for beam in range(beams):
            tile, rest_px = places[beam]
            base = (half + 1) * rows + row - 2 * tile
            here = scratch[beam, pl.ds(base, step), :]
            before = scratch[beam, pl.ds(base - 2, step), :]
            part = jnp.where(lane >= rest_px, here, before)
            result = part if result is None else result + part
        return result

    @pl.when(pl.program_id(0) == 0)
    def _():
        for beam in range(beams):
            for row in range(0, rows, step):
                shift(shifted[0], beam, row, weights_ref[beam, row : row + step, :])
        for half in range(2):
            for row in range(0, rows, step):
                wsum_ref[half, row : row + step, :] = total(shifted[0], half, row)

    for channel in range(block):
        for beam in range(beams):
            for row in range(0, rows, step):
                weight = weights_ref[beam, row : row + step, :]
                value = images_ref[beam, channel, row : row + step, :]
                shift(shifted[channel], beam, row, value * weight)
        for half, outs in enumerate((own, following)):
            for row in range(0, rows, step):
                value = total(shifted[channel], half, row)
                for index in range(step // share):
                    member = row // share + index
                    for out, (begin, count) in zip(outs, spans):
                        first = index * share + begin
                        out[member, channel] = value[first : first + count]


def channel_block(channels):
    return max(size for size in range(1, 5) if channels % size == 0)


def gather(members, spans, starts, weights, images):
    beams, channels, rows, _ = images.shape
    block = channel_block(channels)
    chunks = len(spans)
    result = pl.pallas_call(
        functools.partial(gather_kernel, spans),
        grid_spec=pltpu.PrefetchScalarGridSpec(
            num_scalar_prefetch=1,
            grid=(channels // block,),
            in_specs=[
                pl.BlockSpec((beams, rows, LANES), lambda step, _: (0, 0, 0)),
                pl.BlockSpec((beams, block, rows, LANES), lambda step, _: (0, step, 0, 0)),
            ],
            out_specs=[
                pl.BlockSpec((members, block, count, LANES), lambda step, _: (0, step, 0, 0))
                for _, count in spans
            ]
            * 2
            + [pl.BlockSpec((2, rows, LANES), lambda step, _: (0, 0, 0))],
            scratch_shapes=[pltpu.VMEM((beams, 3 * rows, LANES), jnp.float32)] * block,
        ),
        out_shape=[
            jax.ShapeDtypeStruct((members, channels, count, LANES), jnp.float32)
            for _, count in spans
        ]
        * 2
        + [jax.ShapeDtypeStruct((2, rows, LANES), jnp.float32)],
        compiler_params=pltpu.CompilerParams(vmem_limit_bytes=VMEM),
        name="gather",
    )(starts, weights, images)
    return result[:chunks], result[chunks : 2 * chunks], result[2 * chunks]


def scatter_kernel(spans, offsets_ref, weights_ref, *rest):
    chunks = len(spans)
    own, following = rest[:chunks], rest[chunks : 2 * chunks]
    out_ref, joined = rest[2 * chunks], rest[2 * chunks + 1 :]
    beams, block, rows, _ = out_ref.shape
    members = own[0].shape[0]
    share = rows // members
    step = 64
    lane = lax.broadcasted_iota(jnp.int32, (step, LANES), 1)
    places = [place(offsets_ref, beam) for beam in range(beams)]
    for channel in range(block):
        for half, pieces in enumerate((own, following)):
            for member in range(members):
                for piece, (begin, count) in zip(pieces, spans):
                    row = half * rows + member * share + begin
                    joined[channel][row : row + count, :] = piece[member, channel]
        for beam in range(beams):
            tile, rest_px = places[beam]
            for row in range(0, rows, step):
                base = 2 * tile + row
                here = joined[channel][pl.ds(base, step), :]
                after = joined[channel][pl.ds(base + 2, step), :]
                value = jnp.where(lane >= rest_px, here, after)
                value = pltpu.roll(value, lax.rem(LANES - rest_px, LANES), 1)
                out_ref[beam, channel, row : row + step, :] = (
                    value * weights_ref[beam, row : row + step, :]
                )


def scatter(spans, starts, weights, own, following):
    beams, rows, _ = weights.shape
    members, channels, _, _ = own[0].shape
    block = channel_block(channels)
    return pl.pallas_call(
        functools.partial(scatter_kernel, spans),
        grid_spec=pltpu.PrefetchScalarGridSpec(
            num_scalar_prefetch=1,
            grid=(channels // block,),
            in_specs=[pl.BlockSpec((beams, rows, LANES), lambda step, _: (0, 0, 0))]
            + [
                pl.BlockSpec((members, block, count, LANES), lambda step, _: (0, step, 0, 0))
                for _, count in spans
            ]
            * 2,
            out_specs=pl.BlockSpec((beams, block, rows, LANES), lambda step, _: (0, step, 0, 0)),
            scratch_shapes=[pltpu.VMEM((2 * rows, LANES), jnp.float32)] * block,
        ),
        out_shape=jax.ShapeDtypeStruct((beams, channels, rows, LANES), jnp.float32),
        compiler_params=pltpu.CompilerParams(vmem_limit_bytes=VMEM),
        name="scatter",
    )(starts, weights, *own, *following)


def split(value):
    high = value.astype(jnp.bfloat16)
    return high, (value - high.astype(jnp.float32)).astype(jnp.bfloat16)


def deconvolve_kernel(aliased, groups, *refs):
    if aliased:
        refs = refs[:3] + refs[4:]
    flat_ref, synth_ref, forward_ref, resid_ref, model_ref = refs[:5]
    flat, resid, x, y, product, field = (
        refs[5 + kind * groups : 5 + (kind + 1) * groups] for kind in range(6)
    )
    level = refs[5 + 6 * groups]
    channels = flat[0].shape[0]
    half = field[0].shape[1]
    pixels = field[0].shape[2]
    tiles = pixels // LANES
    stride = 2 * groups * tiles
    sub = 16
    left, right = slice(0, pixels), slice(pixels, 2 * pixels)
    last = lax.broadcasted_iota(jnp.int32, (sub, pixels), 0) == sub - 1

    places = [
        (tile, q, slice(q * pixels + tile * LANES, q * pixels + (tile + 1) * LANES))
        for tile in range(tiles)
        for q in range(2)
    ]

    def feed(group, row, value):
        high, low = split(value)
        for part, piece in enumerate((high, low, high)):
            x[group][part * channels + row : part * channels + row + sub, :] = piece

    def load(group):
        for tile, q, lanes in places:
            flat[group][:, lanes] = flat_ref[
                pl.ds(2 * (group * tiles + tile) + q, channels, stride=stride), :
            ]
        for row in range(0, channels, sub):
            feed(group, row, flat[group][row : row + sub, :])
        extra = x[group].shape[0] - 3 * channels
        x[group][3 * channels :, :] = jnp.zeros((extra, 2 * pixels), jnp.bfloat16)

    def synthesize(group):
        product[group][...] = jnp.dot(
            synth_ref[...], x[group][...], preferred_element_type=jnp.float32
        )

    def project(group):
        resid[group][...] = jnp.dot(
            forward_ref[:, : 4 * half], y[group][...], preferred_element_type=jnp.float32
        ) + jnp.dot(
            forward_ref[:, 4 * half :], y[group][: 2 * half, :], preferred_element_type=jnp.float32
        )

    def step_of(group, row, old):
        rows, low_rows = slice(row, row + sub), slice(half + row, half + row + sub)
        cos_q, cos_u = product[group][rows, left], product[group][rows, right]
        sin_q, sin_u = product[group][low_rows, left], product[group][low_rows, right]
        real_p, real_n = cos_q + sin_u, cos_q - sin_u
        imag_p, imag_n = cos_u - sin_q, cos_u + sin_q
        if row + sub == half:
            real_p = jnp.where(last, product[group][2 * half : 2 * half + 1, left], real_p)
            imag_p = jnp.where(last, product[group][2 * half : 2 * half + 1, right], imag_p)
        values = [real_p, real_n, imag_p, imag_n]
        if old:
            values = [value + field[group][part, rows, :] for part, value in enumerate(values)]
        real_p, real_n, imag_p, imag_n = values
        return values, real_p * real_p + imag_p * imag_p, real_n * real_n + imag_n * imag_n

    def shrink(group, old):
        if not old:
            largest = jnp.zeros((sub, pixels), jnp.float32)
            for row in range(0, half, sub):
                _, power_p, power_n = step_of(group, row, old)
                largest = jnp.maximum(largest, jnp.maximum(power_p, power_n))
            top = jnp.sqrt(jnp.max(largest, axis=0, keepdims=True))
            level[group] = jnp.broadcast_to(
                THRESH_FRAC / STEP_GAIN * top + THRESH_BASE, level.shape[1:]
            )
        limit = level[group]
        for row in range(0, half, sub):
            rows = slice(row, row + sub)
            values, power_p, power_n = step_of(group, row, old)
            factor_p = jnp.maximum(1.0 - limit * lax.rsqrt(power_p), 0.0)
            factor_n = jnp.maximum(1.0 - limit * lax.rsqrt(power_n), 0.0)
            values = [
                value * factor for value, factor in zip(values, (factor_p, factor_n) * 2)
            ]
            for part, value in enumerate(values):
                field[group][part, rows, :] = value
            real_p, real_n, imag_p, imag_n = values
            if row + sub == half:
                real_p, imag_p = jnp.where(last, 0.0, real_p), jnp.where(last, 0.0, imag_p)
            for base, lanes, value in (
                (0, left, real_p + real_n),
                (0, right, imag_p + imag_n),
                (half, left, imag_n - imag_p),
                (half, right, real_p - real_n),
            ):
                high, low = split(value)
                y[group][base + row : base + row + sub, lanes] = high
                y[group][2 * half + base + row : 2 * half + base + row + sub, lanes] = low

    def subtract(group):
        middle = jnp.concatenate(
            [field[group][0, half - 1 : half, :], field[group][2, half - 1 : half, :]], 1
        )
        for row in range(0, channels, sub):
            rows = slice(row, row + sub)
            value = flat[group][rows, :] - (resid[group][rows, :] + middle)
            resid[group][rows, :] = value
            feed(group, row, value)

    def iterate(old):
        for group in range(groups):
            shrink(group, old)
            if group + 1 < groups:
                synthesize(group + 1)
            else:
                project(0)
        for group in range(groups):
            subtract(group)
            if group + 1 < groups:
                project(group + 1)
            else:
                synthesize(0)

    for group in range(groups):
        load(group)
    synthesize(0)
    iterate(False)

    def repeat(number, carry):
        iterate(True)
        return carry

    lax.fori_loop(1, ITERS, repeat, 0)

    for group in range(groups):
        for tile, q, side in places:
            resid_ref[pl.ds(2 * (group * tiles + tile) + q, channels, stride=stride), :] = resid[
                group
            ][:, side]
        lanes = slice(group * pixels, (group + 1) * pixels)
        for part in range(2):
            model_ref[part, half : half + 1, lanes] = field[group][2 * part, half - 1 : half, :]
            model_ref[part, half + 1 :, lanes] = field[group][2 * part, : half - 1, :]

    turn = 32

    def reverse(index, carry):
        row = pl.multiple_of(index * turn, turn)
        for part in range(2):
            value = jnp.concatenate(
                [field[group][2 * part + 1, pl.ds(row, turn), :] for group in range(groups)], 1
            )
            for line in range(turn):
                model_ref[part, pl.ds(half - 1 - line - row, 1), :] = value[line : line + 1, :]
        return carry

    lax.fori_loop(0, half // turn, reverse, 0)


def deconvolve(begin, depths, pixels, cube, synth, forward, model):
    members, group, rows, _ = cube.shape
    channels = members * group
    half = depths // 2
    size = rows // 2 * LANES
    groups = max(1, size // GROUP)
    wide = size // groups
    flat = cube.reshape(channels * rows, LANES)
    whole = pl.BlockSpec(flat.shape, lambda step: (0, 0))
    aliased = model is not None
    resid, model = pl.pallas_call(
        functools.partial(deconvolve_kernel, aliased, groups),
        grid=(1,),
        in_specs=[
            whole,
            pl.BlockSpec(synth.shape, lambda step: (0, 0)),
            pl.BlockSpec(forward.shape, lambda step: (0, 0)),
        ]
        + [pl.BlockSpec(memory_space=pl.ANY)] * aliased,
        out_specs=[whole, pl.BlockSpec((2, depths, size), lambda step: (0, 0, begin // rows))],
        out_shape=[
            jax.ShapeDtypeStruct(flat.shape, jnp.float32),
            jax.ShapeDtypeStruct((2, depths, pixels), jnp.float32),
        ],
        scratch_shapes=[pltpu.VMEM((channels, 2 * wide), jnp.float32)] * (2 * groups)
        + [pltpu.VMEM((synth.shape[1], 2 * wide), jnp.bfloat16)] * groups
        + [pltpu.VMEM((4 * half, 2 * wide), jnp.bfloat16)] * groups
        + [pltpu.VMEM((synth.shape[0], 2 * wide), jnp.float32)] * groups
        + [pltpu.VMEM((4, half, wide), jnp.float32)] * groups
        + [pltpu.VMEM((groups, 16, wide), jnp.float32)],
        input_output_aliases={3: 1} if aliased else {},
        compiler_params=pltpu.CompilerParams(vmem_limit_bytes=VMEM),
        name="deconvolve",
    )(flat, synth, forward, *([model] if aliased else []))
    return resid.reshape(cube.shape), model


def chunk_spans(share):
    if share % 8:
        return ((0, share),)
    return tuple((row, 8) for row in range(0, share, 8))


def body(depths, *arrays):
    return run(depths, *arrays)


def run(depths, beam_images, beam_weights, offsets):
    beams, _, group, tile = beam_images.shape
    members = lax.axis_size("chan")
    sky = lax.axis_size("sky")
    pixels = tile // members
    lines = tile // LANES
    share = 2 * lines // members
    spans = chunk_spans(share)
    channels = group * members
    starts = offsets - lax.axis_index("sky") * tile
    images = beam_images.reshape(beams, 2, group, lines, LANES).transpose(0, 2, 3, 1, 4)
    images = images.reshape(beams, group, 2 * lines, LANES)
    weights = jnp.repeat(beam_weights.reshape(beams, lines, LANES), 2, axis=1)
    forward_pairs = [(index, index + 1) for index in range(sky - 1)]
    backward_pairs = [(index + 1, index) for index in range(sky - 1)]

    own, spill, weight = gather(members, spans, starts, weights, images)
    arrived = []
    for part in spill:
        arrived.append(lax.ppermute(part, "sky", forward_pairs))
    arrived_w = lax.ppermute(weight[1], "sky", forward_pairs)
    scale = (weight[0] + arrived_w + COMBINE_FLOOR).reshape(members, 1, share, LANES)
    synth, forward = depth_tables(channels, depths)

    model = None
    resid, following = [], []
    for chunk, (begin, count) in enumerate(spans):
        combined = (own[chunk] + arrived[chunk]) / scale[:, :, begin : begin + count]
        cube = lax.all_to_all(combined, "chan", 0, 0, tiled=True)
        part, model = deconvolve(begin, depths, pixels, cube, synth, forward, model)
        part = lax.all_to_all(part, "chan", 0, 0, tiled=True)
        resid.append(part)
        following.append(lax.ppermute(part, "sky", backward_pairs))
    outputs = scatter(spans, starts, weights, resid, following)
    outputs = outputs.reshape(beams, group, lines, 2, LANES).transpose(0, 3, 1, 2, 4)
    return outputs.reshape(beam_images.shape), model


DEPTHS = 512


def solution(mesh):
    in_specs = (P("sky", None, "chan", None), P("sky", None), P("sky"))
    out_specs = (P("sky", None, "chan", None), P(None, None, ("sky", "chan")))
    return jax.shard_map(
        functools.partial(body, DEPTHS),
        mesh=mesh,
        in_specs=in_specs,
        out_specs=out_specs,
        check_vma=False,
    )
```

```python
import functools

import jax
import jax.numpy as jnp
from jax import lax
from jax.experimental import pallas as pl
from jax.experimental.pallas import tpu as pltpu
from jax.sharding import PartitionSpec as P


ITERS = 3

BAND_LOW = 800000000.0
BAND_WIDTH = 288000000.0
LIGHT = 299792458.0
DEPTH_STEP = 20.0
COMBINE_FLOOR = 0.5
THRESH_FRAC = 0.25
THRESH_BASE = 0.005
STEP_GAIN = 0.5

LANES = 128
GROUP = 128
VMEM = 60 * 1024 * 1024


def split_rows(arrays):
    high = lax.reduce_precision(arrays, 8, 7)
    return high.astype(jnp.bfloat16), (arrays - high).astype(jnp.bfloat16)


def depth_tables(channels, depths, order):
    half = depths // 2
    channel = jnp.arange(channels, dtype=jnp.float32)
    freq = BAND_LOW + (channel + 0.5) * (BAND_WIDTH / channels)
    lam_sq = (LIGHT / freq) ** 2
    lam_sq = lam_sq - jnp.mean(lam_sq)
    lam_sq = lam_sq.reshape(order.shape[0], -1)[order].reshape(-1)
    depth = (jnp.arange(half, dtype=jnp.float32) + 1.0) * DEPTH_STEP
    angle = 2.0 * depth[:, None] * lam_sq[None, :]
    cosine = jnp.cos(angle)
    sine = jnp.sin(angle)
    ones = jnp.concatenate([jnp.ones((1, channels)), jnp.zeros((15, channels))], 0)
    synth = jnp.concatenate([cosine, sine, ones], 0) / channels * STEP_GAIN
    high, low = split_rows(synth)
    pad = -3 * channels % LANES
    synth = jnp.concatenate([high, high, low, jnp.zeros((high.shape[0], pad), jnp.bfloat16)], 1)
    forward = jnp.concatenate([cosine, sine], 0).T
    high, low = split_rows(forward)
    return synth, jnp.concatenate([high, high, low], 1)


def place(offsets_ref, beam):
    start = offsets_ref[beam]
    return lax.div(start, LANES), lax.rem(start, LANES)


def gather_kernel(spans, offsets_ref, me_ref, weights_ref, images_ref, *rest):
    chunks = len(spans)
    own, keep, give = rest[:2], rest[2 : 2 + chunks], rest[2 + chunks : 2 + 2 * chunks]
    wsum_ref, shifted = rest[2 + 2 * chunks], rest[3 + 2 * chunks :]
    first_core = lax.rem(me_ref[0], 2) == 0
    beams, block, rows, _ = images_ref.shape
    share = own[0].shape[2]
    step = max(64, 2 * share)
    lane = lax.broadcasted_iota(jnp.int32, (step, LANES), 1)
    places = [place(offsets_ref, beam) for beam in range(beams)]

    pixel = lane + LANES * (lax.broadcasted_iota(jnp.int32, (step, LANES), 0) // 2)

    def shift(scratch, beam, row, value):
        value = pltpu.roll(value, places[beam][1], 1)
        scratch[beam, row : row + step, :] = value
        scratch[beam, rows + row : rows + row + step, :] = value

    def total(scratch, row):
        inside = outside = 0.0
        for beam in range(beams):
            tile, rest_px = places[beam]
            base = rows + row - 2 * tile
            here = scratch[beam, pl.ds(base, step), :]
            before = scratch[beam, pl.ds(base - 2, step), :]
            part = jnp.where(lane >= rest_px, here, before)
            own_pixel = pixel >= offsets_ref[beam] - row // 2 * LANES
            inside = inside + jnp.where(own_pixel, part, 0.0)
            outside = outside + jnp.where(own_pixel, 0.0, part)
        return inside, outside

    @pl.when(pl.program_id(0) == 0)
    def _():
        for beam in range(beams):
            for row in range(0, rows, step):
                shift(shifted[0], beam, row, weights_ref[beam, row : row + step, :])
        for row in range(0, rows, step):
            for half, value in enumerate(total(shifted[0], row)):
                wsum_ref[half, row : row + step, :] = value

    def emit(channel, row):
        inside, outside = total(shifted[channel], row)
        for index in range(0, step // share, 2):
            chip = (row // share + index) // 2
            cut = [slice(part * share, (part + 1) * share) for part in (index, index + 1)]
            for side, value in enumerate((inside, outside)):
                same = jnp.where(first_core, value[cut[0]], value[cut[1]])
                other = jnp.where(first_core, value[cut[1]], value[cut[0]])
                if side == 0:
                    own[0][chip, channel], own[1][chip, channel] = same, other
                    continue
                for part, (begin, count) in enumerate(spans):
                    keep[part][chip, channel] = same[begin : begin + count]
                    give[part][chip, channel] = other[begin : begin + count]

    for channel in range(block + 1):
        for row in range(0, rows, step):
            if channel < block:
                for beam in range(beams):
                    weight = weights_ref[beam, row : row + step, :]
                    value = images_ref[beam, channel, row : row + step, :]
                    shift(shifted[channel], beam, row, value * weight)
            if channel:
                emit(channel - 1, row)


def channel_block(channels):
    return max(size for size in range(1, 7) if channels % size == 0)


def gather(chips, spans, starts, me, weights, images):
    beams, channels, rows, _ = images.shape
    block = channel_block(channels)
    chunks = len(spans)
    counts = [rows // (2 * chips)] * 2 + [count for _, count in spans] * 2
    result = pl.pallas_call(
        functools.partial(gather_kernel, spans),
        grid_spec=pltpu.PrefetchScalarGridSpec(
            num_scalar_prefetch=2,
            grid=(channels // block,),
            in_specs=[
                pl.BlockSpec((beams, rows, LANES), lambda step, *_: (0, 0, 0)),
                pl.BlockSpec((beams, block, rows, LANES), lambda step, *_: (0, step, 0, 0)),
            ],
            out_specs=[
                pl.BlockSpec((chips, block, count, LANES), lambda step, *_: (0, step, 0, 0))
                for count in counts
            ]
            + [pl.BlockSpec((2, rows, LANES), lambda step, *_: (0, 0, 0))],
            scratch_shapes=[pltpu.VMEM((beams, 2 * rows, LANES), jnp.float32)] * block,
        ),
        out_shape=[
            jax.ShapeDtypeStruct((chips, channels, count, LANES), jnp.float32) for count in counts
        ]
        + [jax.ShapeDtypeStruct((2, rows, LANES), jnp.float32)],
        compiler_params=pltpu.CompilerParams(vmem_limit_bytes=VMEM),
        name="gather",
    )(starts, me, weights, images)
    return result[:2], result[2 : 2 + chunks], result[2 + chunks : 2 + 2 * chunks], result[-1]


def combine_kernel(first, me_ref, scale_ref, *refs):
    own, arrived, outs = refs[:2], refs[2:4], refs[4:]
    count = outs[0].shape[2]
    rows = slice(first, first + count)
    for index, out in enumerate(outs):
        chip = jnp.bitwise_xor(lax.div(me_ref[0], 2), index)
        scale = 1.0 / scale_ref[chip, rows, :]
        for side in range(2):
            total = own[side][chip, :, rows, :] + arrived[side][chip]
            out[side] = total * scale[None]


def combine(begin, me, scale, own, arrived):
    chips, channels, _, _ = own[0].shape
    count = arrived[0].shape[2]
    tall = max(8, count)
    block = channels // 3
    wide = pl.BlockSpec((chips, block, tall, LANES), lambda step, _: (0, step, begin // tall, 0))
    part = pl.BlockSpec((chips, block, count, LANES), lambda step, _: (0, step, 0, 0))
    return pl.pallas_call(
        functools.partial(combine_kernel, begin % tall),
        grid_spec=pltpu.PrefetchScalarGridSpec(
            num_scalar_prefetch=1,
            grid=(3,),
            in_specs=[pl.BlockSpec((chips, tall, LANES), lambda step, _: (0, begin // tall, 0))]
            + [wide] * 2
            + [part] * 2,
            out_specs=[pl.BlockSpec((2, block, count, LANES), lambda step, _: (0, step, 0, 0))]
            * chips,
        ),
        out_shape=[jax.ShapeDtypeStruct((2, channels, count, LANES), jnp.float32)] * chips,
        compiler_params=pltpu.CompilerParams(vmem_limit_bytes=VMEM),
        name="combine",
    )(me, scale, *own, *arrived)


def scatter_kernel(spans, offsets_ref, weights_ref, *rest):
    chunks = len(spans)
    own, following = rest[:chunks], rest[chunks : 2 * chunks]
    out_ref, joined = rest[2 * chunks], rest[2 * chunks + 1 :]
    beams, block, rows, _ = out_ref.shape
    members = own[0].shape[0]
    share = rows // members
    step = 64
    lane = lax.broadcasted_iota(jnp.int32, (step, LANES), 1)
    places = [place(offsets_ref, beam) for beam in range(beams)]
    for channel in range(block):
        for half, pieces in enumerate((own, following)):
            for member in range(members):
                for piece, (begin, count) in zip(pieces, spans):
                    row = half * rows + member * share + begin
                    joined[channel][row : row + count, :] = piece[member, channel]
        for beam in range(beams):
            tile, rest_px = places[beam]
            for row in range(0, rows, step):
                base = 2 * tile + row
                here = joined[channel][pl.ds(base, step), :]
                after = joined[channel][pl.ds(base + 2, step), :]
                value = jnp.where(lane >= rest_px, here, after)
                value = pltpu.roll(value, lax.rem(LANES - rest_px, LANES), 1)
                out_ref[beam, channel, row : row + step, :] = (
                    value * weights_ref[beam, row : row + step, :]
                )


def scatter(spans, starts, weights, own, following):
    beams, rows, _ = weights.shape
    members, channels, _, _ = own[0].shape
    block = channel_block(channels)
    return pl.pallas_call(
        functools.partial(scatter_kernel, spans),
        grid_spec=pltpu.PrefetchScalarGridSpec(
            num_scalar_prefetch=1,
            grid=(channels // block,),
            in_specs=[pl.BlockSpec((beams, rows, LANES), lambda step, _: (0, 0, 0))]
            + [
                pl.BlockSpec((members, block, count, LANES), lambda step, _: (0, step, 0, 0))
                for _, count in spans
            ]
            * 2,
            out_specs=pl.BlockSpec((beams, block, rows, LANES), lambda step, _: (0, step, 0, 0)),
            scratch_shapes=[pltpu.VMEM((2 * rows, LANES), jnp.float32)] * block,
        ),
        out_shape=jax.ShapeDtypeStruct((beams, channels, rows, LANES), jnp.float32),
        compiler_params=pltpu.CompilerParams(vmem_limit_bytes=VMEM),
        name="scatter",
    )(starts, weights, *own, *following)


def split(value):
    high = value.astype(jnp.bfloat16)
    return high, (value - high.astype(jnp.float32)).astype(jnp.bfloat16)


def deconvolve_kernel(aliased, groups, chips, me_ref, *refs):
    flat_refs, refs = refs[:chips], refs[chips:]
    if aliased:
        refs = refs[:2] + refs[3:]
    synth_ref, forward_ref, resid_ref, model_ref = refs[:4]
    refs = (None, *refs)
    flat, resid, x, y, product, field = (
        refs[5 + kind * groups : 5 + (kind + 1) * groups] for kind in range(6)
    )
    level = refs[5 + 6 * groups]
    channels = flat[0].shape[0]
    half = field[0].shape[1]
    pixels = field[0].shape[2]
    tiles = pixels // LANES
    stride = 2 * groups * tiles
    sub = 16
    left, right = slice(0, pixels), slice(pixels, 2 * pixels)
    last = lax.broadcasted_iota(jnp.int32, (sub, pixels), 0) == sub - 1

    places = [
        (tile, q, slice(q * pixels + tile * LANES, q * pixels + (tile + 1) * LANES))
        for tile in range(tiles)
        for q in range(2)
    ]

    def feed(group, row, value):
        high, low = split(value)
        for part, piece in enumerate((high, low, high)):
            x[group][part * channels + row : part * channels + row + sub, :] = piece

    def load(group):
        for tile, q, lanes in places:
            size = channels // chips
            for chip, ref in enumerate(flat_refs):
                flat[group][chip * size : (chip + 1) * size, lanes] = ref[
                    pl.ds(2 * (group * tiles + tile) + q, size, stride=stride), :
                ]
        for row in range(0, channels, sub):
            feed(group, row, flat[group][row : row + sub, :])
        extra = x[group].shape[0] - 3 * channels
        x[group][3 * channels :, :] = jnp.zeros((extra, 2 * pixels), jnp.bfloat16)

    def synthesize(group):
        product[group][...] = jnp.dot(
            synth_ref[...], x[group][...], preferred_element_type=jnp.float32
        )

    def project(group):
        resid[group][...] = jnp.dot(
            forward_ref[:, : 4 * half], y[group][...], preferred_element_type=jnp.float32
        ) + jnp.dot(
            forward_ref[:, 4 * half :], y[group][: 2 * half, :], preferred_element_type=jnp.float32
        )

    def step_of(group, row, old):
        rows, low_rows = slice(row, row + sub), slice(half + row, half + row + sub)
        cos_q, cos_u = product[group][rows, left], product[group][rows, right]
        sin_q, sin_u = product[group][low_rows, left], product[group][low_rows, right]
        real_p, real_n = cos_q + sin_u, cos_q - sin_u
        imag_p, imag_n = cos_u - sin_q, cos_u + sin_q
        if row + sub == half:
            real_p = jnp.where(last, product[group][2 * half : 2 * half + 1, left], real_p)
            imag_p = jnp.where(last, product[group][2 * half : 2 * half + 1, right], imag_p)
        values = [real_p, real_n, imag_p, imag_n]
        if old:
            values = [value + field[group][part, rows, :] for part, value in enumerate(values)]
        real_p, real_n, imag_p, imag_n = values
        return values, real_p * real_p + imag_p * imag_p, real_n * real_n + imag_n * imag_n

    def shrink(group, old):
        if not old:
            largest = jnp.zeros((sub, pixels), jnp.float32)
            for row in range(0, half, sub):
                _, power_p, power_n = step_of(group, row, old)
                largest = jnp.maximum(largest, jnp.maximum(power_p, power_n))
            top = jnp.sqrt(jnp.max(largest, axis=0, keepdims=True))
            level[group] = jnp.broadcast_to(
                THRESH_FRAC / STEP_GAIN * top + THRESH_BASE, level.shape[1:]
            )
        limit = level[group]
        for row in range(0, half, sub):
            rows = slice(row, row + sub)
            values, power_p, power_n = step_of(group, row, old)
            factor_p = jnp.maximum(1.0 - limit * lax.rsqrt(power_p), 0.0)
            factor_n = jnp.maximum(1.0 - limit * lax.rsqrt(power_n), 0.0)
            values = [
                value * factor for value, factor in zip(values, (factor_p, factor_n) * 2)
            ]
            for part, value in enumerate(values):
                field[group][part, rows, :] = value
            real_p, real_n, imag_p, imag_n = values
            if row + sub == half:
                real_p, imag_p = jnp.where(last, 0.0, real_p), jnp.where(last, 0.0, imag_p)
            for base, lanes, value in (
                (0, left, real_p + real_n),
                (0, right, imag_p + imag_n),
                (half, left, imag_n - imag_p),
                (half, right, real_p - real_n),
            ):
                high, low = split(value)
                y[group][base + row : base + row + sub, lanes] = high
                y[group][2 * half + base + row : 2 * half + base + row + sub, lanes] = low

    def subtract(group):
        middle = jnp.concatenate(
            [field[group][0, half - 1 : half, :], field[group][2, half - 1 : half, :]], 1
        )
        for row in range(0, channels, sub):
            rows = slice(row, row + sub)
            value = flat[group][rows, :] - (resid[group][rows, :] + middle)
            resid[group][rows, :] = value
            feed(group, row, value)

    def iterate(old):
        for group in range(groups):
            shrink(group, old)
            if group + 1 < groups:
                synthesize(group + 1)
            else:
                project(0)
        for group in range(groups):
            subtract(group)
            if group + 1 < groups:
                project(group + 1)
            else:
                synthesize(0)

    for group in range(groups):
        load(group)
    synthesize(0)
    iterate(False)

    def repeat(number, carry):
        iterate(True)
        return carry

    lax.fori_loop(1, ITERS, repeat, 0)

    for group in range(groups):
        for tile, q, side in places:
            size = channels // (2 * chips)
            for part in range(2 * chips):
                base = jnp.bitwise_xor(me_ref[0], part) * (size * stride)
                base = base + (2 * (group * tiles + tile) + q)
                resid_ref[pl.ds(base, size, stride=stride), :] = resid[group][
                    part * size : (part + 1) * size, side
                ]
        lanes = slice(group * pixels, (group + 1) * pixels)
        for part in range(2):
            model_ref[part, half : half + 1, lanes] = field[group][2 * part, half - 1 : half, :]
            model_ref[part, half + 1 :, lanes] = field[group][2 * part, : half - 1, :]

    turn = 32

    def reverse(index, carry):
        row = pl.multiple_of(index * turn, turn)
        for part in range(2):
            value = jnp.concatenate(
                [field[group][2 * part + 1, pl.ds(row, turn), :] for group in range(groups)], 1
            )
            for line in range(turn):
                model_ref[part, pl.ds(half - 1 - line - row, 1), :] = value[line : line + 1, :]
        return carry

    lax.fori_loop(0, half // turn, reverse, 0)


def deconvolve(begin, depths, pixels, me, cube, synth, forward, model):
    chips = len(cube)
    _, group, rows, _ = cube[0].shape
    channels = 2 * chips * group
    half = depths // 2
    size = rows // 2 * LANES
    groups = max(1, size // GROUP)
    wide = size // groups
    cube = [part.reshape(-1, LANES) for part in cube]
    whole = (channels * rows, LANES)
    aliased = model is not None
    resid, model = pl.pallas_call(
        functools.partial(deconvolve_kernel, aliased, groups, chips),
        grid_spec=pltpu.PrefetchScalarGridSpec(
            num_scalar_prefetch=1,
            grid=(1,),
            in_specs=[pl.BlockSpec(part.shape, lambda step, _: (0, 0)) for part in cube]
            + [
                pl.BlockSpec(synth.shape, lambda step, _: (0, 0)),
                pl.BlockSpec(forward.shape, lambda step, _: (0, 0)),
            ]
            + [pl.BlockSpec(memory_space=pl.ANY)] * aliased,
            out_specs=[
                pl.BlockSpec(whole, lambda step, _: (0, 0)),
                pl.BlockSpec((2, depths, size), lambda step, _: (0, 0, begin // rows)),
            ],
            scratch_shapes=[pltpu.VMEM((channels, 2 * wide), jnp.float32)] * (2 * groups)
            + [pltpu.VMEM((synth.shape[1], 2 * wide), jnp.bfloat16)] * groups
            + [pltpu.VMEM((4 * half, 2 * wide), jnp.bfloat16)] * groups
            + [pltpu.VMEM((synth.shape[0], 2 * wide), jnp.float32)] * groups
            + [pltpu.VMEM((4, half, wide), jnp.float32)] * groups
            + [pltpu.VMEM((groups, 16, wide), jnp.float32)],
        ),
        out_shape=[
            jax.ShapeDtypeStruct(whole, jnp.float32),
            jax.ShapeDtypeStruct((2, depths, pixels), jnp.float32),
        ],
        input_output_aliases={3 + chips: 1} if aliased else {},
        compiler_params=pltpu.CompilerParams(vmem_limit_bytes=VMEM),
        name="deconvolve",
    )(me, *cube, synth, forward, *([model] if aliased else []))
    return resid.reshape(2 * chips, group, rows, LANES), model


def chunk_spans(share):
    if share % 8 or share < 32:
        return ((0, share),)
    return ((0, 4), *((row, 8) for row in range(8, share, 8)), (4, 4))


def body(depths, *arrays):
    return run(depths, *arrays)


def run(depths, beam_images, beam_weights, offsets):
    beams, _, group, tile = beam_images.shape
    members = lax.axis_size("chan")
    sky = lax.axis_size("sky")
    pixels = tile // members
    lines = tile // LANES
    share = 2 * lines // members
    spans = chunk_spans(share)
    channels = group * members
    starts = offsets - lax.axis_index("sky") * tile
    images = beam_images.reshape(beams, 2, group, lines, LANES).transpose(0, 2, 3, 1, 4)
    images = images.reshape(beams, group, 2 * lines, LANES)
    weights = jnp.repeat(beam_weights.reshape(beams, lines, LANES), 2, axis=1)
    chips = members // 2
    me = lax.axis_index("chan").astype(jnp.int32)
    mine = me.reshape(1)
    ahead = [
        [(t * members + c, (t + 1) * members + (c ^ other)) for t in range(sky - 1) for c in range(members)]
        for other in range(2)
    ]
    backward_pairs = [(index + 1, index) for index in range(sky - 1)]
    both = ("sky", "chan")

    own, keep, give, weight = gather(chips, spans, starts, mine, weights, images)
    arrived = []
    for chunk in range(len(spans)):
        straight = lax.ppermute(keep[chunk], both, ahead[0])
        arrived.append((straight, lax.ppermute(give[chunk], both, ahead[1])))
    crossed = lax.ppermute(own[1], "chan", [(c, c ^ 1) for c in range(members)])
    arrived_w = lax.ppermute(weight[1], both, ahead[0])
    scale = (weight[0] + arrived_w + COMBINE_FLOOR).reshape(chips, 2, share, LANES)
    scale = lax.dynamic_index_in_dim(scale, lax.rem(me, 2), 1, keepdims=False)
    order = jnp.bitwise_xor(me, jnp.arange(members, dtype=jnp.int32))
    synth, forward = depth_tables(channels, depths, order)

    model = None
    resid, following = [], []
    for chunk, (begin, count) in enumerate(spans):
        cube = list(combine(begin, mine, scale, (own[0], crossed), arrived[chunk]))
        for index in range(1, chips):
            pairs = [(c, c ^ (2 * index)) for c in range(members)]
            cube[index] = lax.ppermute(cube[index], "chan", pairs)
        part, model = deconvolve(begin, depths, pixels, mine, cube, synth, forward, model)
        part = lax.all_to_all(part, "chan", 0, 0, tiled=True)
        resid.append(part)
        following.append(lax.ppermute(part, "sky", backward_pairs))
    outputs = scatter(spans, starts, weights, resid, following)
    outputs = outputs.reshape(beams, group, lines, 2, LANES).transpose(0, 3, 1, 2, 4)
    return outputs.reshape(beam_images.shape), model


DEPTHS = 512


def solution(mesh):
    in_specs = (P("sky", None, "chan", None), P("sky", None), P("sky"))
    out_specs = (P("sky", None, "chan", None), P(None, None, ("sky", "chan")))
    return jax.shard_map(
        functools.partial(body, DEPTHS),
        mesh=mesh,
        in_specs=in_specs,
        out_specs=out_specs,
        check_vma=False,
    )
```

```python
import functools

import jax
import jax.numpy as jnp
from jax import lax
from jax.experimental import pallas as pl
from jax.experimental.pallas import tpu as pltpu
from jax.sharding import PartitionSpec as P


ITERS = 3

BAND_LOW = 800000000.0
BAND_WIDTH = 288000000.0
LIGHT = 299792458.0
DEPTH_STEP = 20.0
COMBINE_FLOOR = 0.5
THRESH_FRAC = 0.25
THRESH_BASE = 0.005
STEP_GAIN = 0.5

LANES = 128
GROUP = 128
VMEM = 67043328


def split_rows(arrays):
    high = lax.reduce_precision(arrays, 8, 7)
    return high.astype(jnp.bfloat16), (arrays - high).astype(jnp.bfloat16)


def depth_tables(channels, depths, order):
    half = depths // 2
    channel = jnp.arange(channels, dtype=jnp.float32)
    freq = BAND_LOW + (channel + 0.5) * (BAND_WIDTH / channels)
    lam_sq = (LIGHT / freq) ** 2
    lam_sq = lam_sq - jnp.mean(lam_sq)
    lam_sq = lam_sq.reshape(order.shape[0], -1)[order].reshape(-1)
    depth = (jnp.arange(half, dtype=jnp.float32) + 1.0) * DEPTH_STEP
    angle = 2.0 * depth[:, None] * lam_sq[None, :]
    cosine = jnp.cos(angle)
    sine = jnp.sin(angle)
    ones = jnp.concatenate([jnp.ones((1, channels)), jnp.zeros((15, channels))], 0)
    synth = jnp.concatenate([cosine, sine, ones], 0) / channels * STEP_GAIN
    high, low = split_rows(synth)
    pad = -3 * channels % LANES
    synth = jnp.concatenate([high, high, low, jnp.zeros((high.shape[0], pad), jnp.bfloat16)], 1)
    forward = jnp.concatenate([cosine, sine], 0).T
    high, low = split_rows(forward)
    return synth, jnp.concatenate([high, high, low], 1)


def place(offsets_ref, beam):
    start = offsets_ref[beam]
    return lax.div(start, LANES), lax.rem(start, LANES)


def gather_kernel(spans, offsets_ref, me_ref, weights_ref, images_ref, *rest):
    chunks = len(spans)
    own, keep, give = rest[:2], rest[2 : 2 + chunks], rest[2 + chunks : 2 + 2 * chunks]
    wsum_refs, shifted = rest[2 + 2 * chunks : 4 + 2 * chunks], rest[4 + 2 * chunks :]
    first_core = lax.rem(me_ref[0], 2) == 0
    beams, block, rows, _ = images_ref.shape
    share = own[0].shape[2]
    step = max(64, 2 * share)
    lane = lax.broadcasted_iota(jnp.int32, (step, LANES), 1)
    places = [place(offsets_ref, beam) for beam in range(beams)]

    pixel = lane + LANES * (lax.broadcasted_iota(jnp.int32, (step, LANES), 0) // 2)

    def shift(scratch, beam, row, value):
        value = pltpu.roll(value, places[beam][1], 1)
        scratch[beam, row : row + step, :] = value
        scratch[beam, rows + row : rows + row + step, :] = value

    def total(scratch, row):
        inside = outside = 0.0
        for beam in range(beams):
            tile, rest_px = places[beam]
            base = rows + row - 2 * tile
            here = scratch[beam, pl.ds(base, step), :]
            before = scratch[beam, pl.ds(base - 2, step), :]
            part = jnp.where(lane >= rest_px, here, before)
            own_pixel = pixel >= offsets_ref[beam] - row // 2 * LANES
            inside = inside + jnp.where(own_pixel, part, 0.0)
            outside = outside + jnp.where(own_pixel, 0.0, part)
        return inside, outside

    @pl.when(pl.program_id(0) == 0)
    def _():
        for beam in range(beams):
            for row in range(0, rows, step):
                shift(shifted[0], beam, row, weights_ref[beam, row : row + step, :])
        for row in range(0, rows, step):
            for wsum_ref, value in zip(wsum_refs, total(shifted[0], row)):
                wsum_ref[row : row + step, :] = value

    def emit(channel, row):
        inside, outside = total(shifted[channel], row)
        for index in range(0, step // share, 2):
            chip = (row // share + index) // 2
            cut = [slice(part * share, (part + 1) * share) for part in (index, index + 1)]
            for side, value in enumerate((inside, outside)):
                same = jnp.where(first_core, value[cut[0]], value[cut[1]])
                other = jnp.where(first_core, value[cut[1]], value[cut[0]])
                if side == 0:
                    own[0][chip, channel], own[1][chip, channel] = same, other
                    continue
                for part, (begin, count) in enumerate(spans):
                    keep[part][chip, channel] = same[begin : begin + count]
                    give[part][chip, channel] = other[begin : begin + count]

    for channel in range(block + 1):
        for row in range(0, rows, step):
            if channel < block:
                for beam in range(beams):
                    weight = weights_ref[beam, row : row + step, :]
                    value = images_ref[beam, channel, row : row + step, :]
                    shift(shifted[channel], beam, row, value * weight)
            if channel:
                emit(channel - 1, row)


def channel_block(channels):
    return max(size for size in range(1, 7) if channels % size == 0)


def gather(chips, spans, starts, me, weights, images):
    beams, channels, rows, _ = images.shape
    block = channel_block(channels)
    chunks = len(spans)
    counts = [rows // (2 * chips)] * 2 + [count for _, count in spans] * 2
    result = pl.pallas_call(
        functools.partial(gather_kernel, spans),
        grid_spec=pltpu.PrefetchScalarGridSpec(
            num_scalar_prefetch=2,
            grid=(channels // block,),
            in_specs=[
                pl.BlockSpec((beams, rows, LANES), lambda step, *_: (0, 0, 0)),
                pl.BlockSpec((beams, block, rows, LANES), lambda step, *_: (0, step, 0, 0)),
            ],
            out_specs=[
                pl.BlockSpec((chips, block, count, LANES), lambda step, *_: (0, step, 0, 0))
                for count in counts
            ]
            + [pl.BlockSpec((rows, LANES), lambda step, *_: (0, 0))] * 2,
            scratch_shapes=[pltpu.VMEM((beams, 2 * rows, LANES), jnp.float32)] * block,
        ),
        out_shape=[
            jax.ShapeDtypeStruct((chips, channels, count, LANES), jnp.float32) for count in counts
        ]
        + [jax.ShapeDtypeStruct((rows, LANES), jnp.float32)] * 2,
        compiler_params=pltpu.CompilerParams(vmem_limit_bytes=VMEM),
        name="gather",
    )(starts, me, weights, images)
    return result[:2], result[2 : 2 + chunks], result[2 + chunks : 2 + 2 * chunks], result[-2:]


def combine_kernel(first, me_ref, scale_ref, *refs):
    own, arrived, outs = refs[:2], refs[2:4], refs[4:]
    count = outs[0].shape[2]
    rows = slice(first, first + count)
    for index, out in enumerate(outs):
        chip = jnp.bitwise_xor(lax.div(me_ref[0], 2), index)
        scale = 1.0 / scale_ref[chip, rows, :]
        for side in range(2):
            total = own[side][chip, :, rows, :] + arrived[side][chip]
            out[side] = total * scale[None]


def combine(begin, me, scale, own, arrived):
    chips, channels, _, _ = own[0].shape
    count = arrived[0].shape[2]
    tall = max(8, count)
    block = channels // 3
    wide = pl.BlockSpec((chips, block, tall, LANES), lambda step, _: (0, step, begin // tall, 0))
    part = pl.BlockSpec((chips, block, count, LANES), lambda step, _: (0, step, 0, 0))
    return pl.pallas_call(
        functools.partial(combine_kernel, begin % tall),
        grid_spec=pltpu.PrefetchScalarGridSpec(
            num_scalar_prefetch=1,
            grid=(3,),
            in_specs=[pl.BlockSpec((chips, tall, LANES), lambda step, _: (0, begin // tall, 0))]
            + [wide] * 2
            + [part] * 2,
            out_specs=[pl.BlockSpec((2, block, count, LANES), lambda step, _: (0, step, 0, 0))]
            * chips,
        ),
        out_shape=[jax.ShapeDtypeStruct((2, channels, count, LANES), jnp.float32)] * chips,
        compiler_params=pltpu.CompilerParams(vmem_limit_bytes=VMEM),
        name="combine",
    )(me, scale, *own, *arrived)


def scatter_kernel(spans, offsets_ref, weights_ref, *rest):
    chunks = len(spans)
    own, following = rest[:chunks], rest[chunks : 2 * chunks]
    out_ref, joined = rest[2 * chunks], rest[2 * chunks + 1 :]
    beams, block, rows, _ = out_ref.shape
    members = own[0].shape[0]
    share = rows // members
    step = 64
    lane = lax.broadcasted_iota(jnp.int32, (step, LANES), 1)
    places = [place(offsets_ref, beam) for beam in range(beams)]
    for channel in range(block):
        for half, pieces in enumerate((own, following)):
            for member in range(members):
                for piece, (begin, count) in zip(pieces, spans):
                    row = half * rows + member * share + begin
                    joined[channel][row : row + count, :] = piece[member, channel]
        for beam in range(beams):
            tile, rest_px = places[beam]
            for row in range(0, rows, step):
                base = 2 * tile + row
                here = joined[channel][pl.ds(base, step), :]
                after = joined[channel][pl.ds(base + 2, step), :]
                value = jnp.where(lane >= rest_px, here, after)
                value = pltpu.roll(value, lax.rem(LANES - rest_px, LANES), 1)
                out_ref[beam, channel, row : row + step, :] = (
                    value * weights_ref[beam, row : row + step, :]
                )


def scatter(spans, starts, weights, own, following):
    beams, rows, _ = weights.shape
    members, channels, _, _ = own[0].shape
    block = channel_block(channels)
    return pl.pallas_call(
        functools.partial(scatter_kernel, spans),
        grid_spec=pltpu.PrefetchScalarGridSpec(
            num_scalar_prefetch=1,
            grid=(channels // block,),
            in_specs=[pl.BlockSpec((beams, rows, LANES), lambda step, _: (0, 0, 0))]
            + [
                pl.BlockSpec((members, block, count, LANES), lambda step, _: (0, step, 0, 0))
                for _, count in spans
            ]
            * 2,
            out_specs=pl.BlockSpec((beams, block, rows, LANES), lambda step, _: (0, step, 0, 0)),
            scratch_shapes=[pltpu.VMEM((2 * rows, LANES), jnp.float32)] * block,
        ),
        out_shape=jax.ShapeDtypeStruct((beams, channels, rows, LANES), jnp.float32),
        compiler_params=pltpu.CompilerParams(vmem_limit_bytes=VMEM),
        name="scatter",
    )(starts, weights, *own, *following)


def split(value):
    high = value.astype(jnp.bfloat16)
    return high, (value - high.astype(jnp.float32)).astype(jnp.bfloat16)


def deconvolve_kernel(aliased, groups, chips, me_ref, *refs):
    flat_refs, refs = refs[:chips], refs[chips:]
    if aliased:
        refs = refs[:2] + refs[3:]
    synth_ref, forward_ref, resid_ref, model_ref = refs[:4]
    refs = (None, *refs)
    flat, resid, x, y, product, field = (
        refs[5 + kind * groups : 5 + (kind + 1) * groups] for kind in range(6)
    )
    level = refs[5 + 6 * groups]
    channels = flat[0].shape[0]
    half = field[0].shape[1]
    pixels = field[0].shape[2]
    tiles = pixels // LANES
    stride = 2 * groups * tiles
    sub = 16
    left, right = slice(0, pixels), slice(pixels, 2 * pixels)
    last = lax.broadcasted_iota(jnp.int32, (sub, pixels), 0) == sub - 1

    places = [
        (tile, q, slice(q * pixels + tile * LANES, q * pixels + (tile + 1) * LANES))
        for tile in range(tiles)
        for q in range(2)
    ]

    def feed(group, row, value):
        high, low = split(value)
        for part, piece in enumerate((high, low, high)):
            x[group][part * channels + row : part * channels + row + sub, :] = piece

    def load(group):
        for tile, q, lanes in places:
            size = channels // chips
            for chip, ref in enumerate(flat_refs):
                flat[group][chip * size : (chip + 1) * size, lanes] = ref[
                    pl.ds(2 * (group * tiles + tile) + q, size, stride=stride), :
                ]
        for row in range(0, channels, sub):
            feed(group, row, flat[group][row : row + sub, :])
        extra = x[group].shape[0] - 3 * channels
        x[group][3 * channels :, :] = jnp.zeros((extra, 2 * pixels), jnp.bfloat16)

    def synthesize(group):
        product[group][...] = jnp.dot(
            synth_ref[...], x[group][...], preferred_element_type=jnp.float32
        )

    def project(group):
        resid[group][...] = jnp.dot(
            forward_ref[:, : 4 * half], y[group][...], preferred_element_type=jnp.float32
        ) + jnp.dot(
            forward_ref[:, 4 * half :], y[group][: 2 * half, :], preferred_element_type=jnp.float32
        )

    def step_of(group, row, old):
        rows, low_rows = slice(row, row + sub), slice(half + row, half + row + sub)
        cos_q, cos_u = product[group][rows, left], product[group][rows, right]
        sin_q, sin_u = product[group][low_rows, left], product[group][low_rows, right]
        real_p, real_n = cos_q + sin_u, cos_q - sin_u
        imag_p, imag_n = cos_u - sin_q, cos_u + sin_q
        if row + sub == half:
            real_p = jnp.where(last, product[group][2 * half : 2 * half + 1, left], real_p)
            imag_p = jnp.where(last, product[group][2 * half : 2 * half + 1, right], imag_p)
        values = [real_p, real_n, imag_p, imag_n]
        if old:
            values = [value + field[group][part, rows, :] for part, value in enumerate(values)]
        real_p, real_n, imag_p, imag_n = values
        return values, real_p * real_p + imag_p * imag_p, real_n * real_n + imag_n * imag_n

    def shrink(group, old):
        if not old:
            largest = jnp.zeros((sub, pixels), jnp.float32)
            for row in range(0, half, sub):
                _, power_p, power_n = step_of(group, row, old)
                largest = jnp.maximum(largest, jnp.maximum(power_p, power_n))
            top = jnp.sqrt(jnp.max(largest, axis=0, keepdims=True))
            level[group] = jnp.broadcast_to(
                THRESH_FRAC / STEP_GAIN * top + THRESH_BASE, level.shape[1:]
            )
        limit = level[group]
        for row in range(0, half, sub):
            rows = slice(row, row + sub)
            values, power_p, power_n = step_of(group, row, old)
            factor_p = jnp.maximum(1.0 - limit * lax.rsqrt(power_p), 0.0)
            factor_n = jnp.maximum(1.0 - limit * lax.rsqrt(power_n), 0.0)
            values = [
                value * factor for value, factor in zip(values, (factor_p, factor_n) * 2)
            ]
            for part, value in enumerate(values):
                field[group][part, rows, :] = value
            real_p, real_n, imag_p, imag_n = values
            if row + sub == half:
                real_p, imag_p = jnp.where(last, 0.0, real_p), jnp.where(last, 0.0, imag_p)
            for base, lanes, value in (
                (0, left, real_p + real_n),
                (0, right, imag_p + imag_n),
                (half, left, imag_n - imag_p),
                (half, right, real_p - real_n),
            ):
                high, low = split(value)
                y[group][base + row : base + row + sub, lanes] = high
                y[group][2 * half + base + row : 2 * half + base + row + sub, lanes] = low

    def subtract(group):
        middle = jnp.concatenate(
            [field[group][0, half - 1 : half, :], field[group][2, half - 1 : half, :]], 1
        )
        for row in range(0, channels, sub):
            rows = slice(row, row + sub)
            value = flat[group][rows, :] - (resid[group][rows, :] + middle)
            resid[group][rows, :] = value
            feed(group, row, value)

    def iterate(old):
        for group in range(groups):
            shrink(group, old)
            if group + 1 < groups:
                synthesize(group + 1)
            else:
                project(0)
        for group in range(groups):
            subtract(group)
            if group + 1 < groups:
                project(group + 1)
            else:
                synthesize(0)

    for group in range(groups):
        load(group)
    synthesize(0)
    iterate(False)

    def repeat(number, carry):
        iterate(True)
        return carry

    lax.fori_loop(1, ITERS, repeat, 0)

    for group in range(groups):
        for tile, q, side in places:
            size = channels // (2 * chips)
            for part in range(2 * chips):
                base = jnp.bitwise_xor(me_ref[0], part) * (size * stride)
                base = base + (2 * (group * tiles + tile) + q)
                resid_ref[pl.ds(base, size, stride=stride), :] = resid[group][
                    part * size : (part + 1) * size, side
                ]
        lanes = slice(group * pixels, (group + 1) * pixels)
        for part in range(2):
            model_ref[part, half : half + 1, lanes] = field[group][2 * part, half - 1 : half, :]
            model_ref[part, half + 1 :, lanes] = field[group][2 * part, : half - 1, :]

    turn = 32

    def reverse(index, carry):
        row = pl.multiple_of(index * turn, turn)
        for part in range(2):
            value = jnp.concatenate(
                [field[group][2 * part + 1, pl.ds(row, turn), :] for group in range(groups)], 1
            )
            for line in range(turn):
                model_ref[part, pl.ds(half - 1 - line - row, 1), :] = value[line : line + 1, :]
        return carry

    lax.fori_loop(0, half // turn, reverse, 0)


def deconvolve(begin, depths, pixels, me, cube, synth, forward, model):
    chips = len(cube)
    _, group, rows, _ = cube[0].shape
    channels = 2 * chips * group
    half = depths // 2
    size = rows // 2 * LANES
    groups = max(1, size // GROUP)
    wide = size // groups
    cube = [part.reshape(-1, LANES) for part in cube]
    whole = (channels * rows, LANES)
    aliased = model is not None
    resid, model = pl.pallas_call(
        functools.partial(deconvolve_kernel, aliased, groups, chips),
        grid_spec=pltpu.PrefetchScalarGridSpec(
            num_scalar_prefetch=1,
            grid=(1,),
            in_specs=[pl.BlockSpec(part.shape, lambda step, _: (0, 0)) for part in cube]
            + [
                pl.BlockSpec(synth.shape, lambda step, _: (0, 0)),
                pl.BlockSpec(forward.shape, lambda step, _: (0, 0)),
            ]
            + [pl.BlockSpec(memory_space=pl.ANY)] * aliased,
            out_specs=[
                pl.BlockSpec(whole, lambda step, _: (0, 0)),
                pl.BlockSpec((2, depths, size), lambda step, _: (0, 0, begin // rows)),
            ],
            scratch_shapes=[pltpu.VMEM((channels, 2 * wide), jnp.float32)] * (2 * groups)
            + [pltpu.VMEM((synth.shape[1], 2 * wide), jnp.bfloat16)] * groups
            + [pltpu.VMEM((4 * half, 2 * wide), jnp.bfloat16)] * groups
            + [pltpu.VMEM((synth.shape[0], 2 * wide), jnp.float32)] * groups
            + [pltpu.VMEM((4, half, wide), jnp.float32)] * groups
            + [pltpu.VMEM((groups, 16, wide), jnp.float32)],
        ),
        out_shape=[
            jax.ShapeDtypeStruct(whole, jnp.float32),
            jax.ShapeDtypeStruct((2, depths, pixels), jnp.float32),
        ],
        input_output_aliases={3 + chips: 1} if aliased else {},
        compiler_params=pltpu.CompilerParams(vmem_limit_bytes=VMEM),
        name="deconvolve",
    )(me, *cube, synth, forward, *([model] if aliased else []))
    return resid.reshape(2 * chips, group, rows, LANES), model


def chunk_spans(share):
    if share % 8 or share < 32:
        return ((0, share),)
    return ((0, 4), *((row, 8) for row in range(8, share, 8)), (4, 4))


def body(depths, *arrays):
    return run(depths, *arrays)


def run(depths, beam_images, beam_weights, offsets):
    beams, _, group, tile = beam_images.shape
    members = lax.axis_size("chan")
    sky = lax.axis_size("sky")
    pixels = tile // members
    lines = tile // LANES
    share = 2 * lines // members
    spans = chunk_spans(share)
    channels = group * members
    starts = offsets - lax.axis_index("sky") * tile
    images = beam_images.reshape(beams, 2, group, lines, LANES).transpose(0, 2, 3, 1, 4)
    images = images.reshape(beams, group, 2 * lines, LANES)
    weights = jnp.repeat(beam_weights.reshape(beams, lines, LANES), 2, axis=1)
    chips = members // 2
    me = lax.axis_index("chan").astype(jnp.int32)
    mine = me.reshape(1)
    ahead = [
        [(t * members + c, (t + 1) * members + (c ^ other)) for t in range(sky - 1) for c in range(members)]
        for other in range(2)
    ]
    backward_pairs = [(index + 1, index) for index in range(sky - 1)]
    both = ("sky", "chan")

    own, keep, give, weight = gather(chips, spans, starts, mine, weights, images)
    arrived = []
    for chunk in range(len(spans)):
        straight = lax.ppermute(keep[chunk], both, ahead[0])
        arrived.append((straight, lax.ppermute(give[chunk], both, ahead[1])))
    crossed = lax.ppermute(own[1], "chan", [(c, c ^ 1) for c in range(members)])
    arrived_w = lax.ppermute(weight[1], both, ahead[0])
    scale = (weight[0] + arrived_w + COMBINE_FLOOR).reshape(chips, 2, share, LANES)
    scale = lax.dynamic_index_in_dim(scale, lax.rem(me, 2), 1, keepdims=False)
    order = jnp.bitwise_xor(me, jnp.arange(members, dtype=jnp.int32))
    synth, forward = depth_tables(channels, depths, order)

    model = None
    resid, following = [], []
    for chunk, (begin, count) in enumerate(spans):
        cube = list(combine(begin, mine, scale, (own[0], crossed), arrived[chunk]))
        for index in range(1, chips):
            pairs = [(c, c ^ (2 * index)) for c in range(members)]
            cube[index] = lax.ppermute(cube[index], "chan", pairs)
        part, model = deconvolve(begin, depths, pixels, mine, cube, synth, forward, model)
        part = lax.all_to_all(part, "chan", 0, 0, tiled=True)
        resid.append(part)
        following.append(lax.ppermute(part, "sky", backward_pairs))
    outputs = scatter(spans, starts, weights, resid, following)
    outputs = outputs.reshape(beams, group, lines, 2, LANES).transpose(0, 3, 1, 2, 4)
    return outputs.reshape(beam_images.shape), model


DEPTHS = 512


def solution(mesh):
    in_specs = (P("sky", None, "chan", None), P("sky", None), P("sky"))
    out_specs = (P("sky", None, "chan", None), P(None, None, ("sky", "chan")))
    return jax.shard_map(
        functools.partial(body, DEPTHS),
        mesh=mesh,
        in_specs=in_specs,
        out_specs=out_specs,
        check_vma=False,
    )
```

```python
import functools

import jax
import jax.numpy as jnp
from jax import lax
from jax.experimental import pallas as pl
from jax.experimental.pallas import tpu as pltpu
from jax.sharding import PartitionSpec as P


ITERS = 3

BAND_LOW = 800000000.0
BAND_WIDTH = 288000000.0
LIGHT = 299792458.0
DEPTH_STEP = 20.0
COMBINE_FLOOR = 0.5
THRESH_FRAC = 0.25
THRESH_BASE = 0.005
STEP_GAIN = 0.5

LANES = 128
GROUP = 128
VMEM = 67043328


def split_rows(arrays):
    high = lax.reduce_precision(arrays, 8, 7)
    return high.astype(jnp.bfloat16), (arrays - high).astype(jnp.bfloat16)


def depth_tables(channels, depths, order):
    half = depths // 2
    channel = jnp.arange(channels, dtype=jnp.float32)
    freq = BAND_LOW + (channel + 0.5) * (BAND_WIDTH / channels)
    lam_sq = (LIGHT / freq) ** 2
    lam_sq = lam_sq - jnp.mean(lam_sq)
    lam_sq = lam_sq.reshape(order.shape[0], -1)[order].reshape(-1)
    depth = (jnp.arange(half, dtype=jnp.float32) + 1.0) * DEPTH_STEP
    angle = 2.0 * depth[:, None] * lam_sq[None, :]
    cosine = jnp.cos(angle)
    sine = jnp.sin(angle)
    ones = jnp.concatenate([jnp.ones((1, channels)), jnp.zeros((15, channels))], 0)
    synth = jnp.concatenate([cosine, sine, ones], 0) / channels * STEP_GAIN
    high, low = split_rows(synth)
    pad = -3 * channels % LANES
    synth = jnp.concatenate([high, high, low, jnp.zeros((high.shape[0], pad), jnp.bfloat16)], 1)
    forward = jnp.concatenate([cosine, sine], 0).T
    high, low = split_rows(forward)
    return synth, jnp.concatenate([high, high, low], 1)


def place(offsets_ref, beam):
    start = offsets_ref[beam]
    return lax.div(start, LANES), lax.rem(start, LANES)


def gather_kernel(spans, offsets_ref, me_ref, weights_ref, images_ref, *rest):
    chunks = len(spans)
    own, keep, give = rest[:2], rest[2 : 2 + chunks], rest[2 + chunks : 2 + 2 * chunks]
    wsum_refs, shifted = rest[2 + 2 * chunks : 4 + 2 * chunks], rest[4 + 2 * chunks :]
    first_core = lax.rem(me_ref[0], 2) == 0
    beams, block, rows, _ = images_ref.shape
    share = own[0].shape[2]
    step = max(64, 2 * share)
    lane = lax.broadcasted_iota(jnp.int32, (step, LANES), 1)
    places = [place(offsets_ref, beam) for beam in range(beams)]

    pixel = lane + LANES * (lax.broadcasted_iota(jnp.int32, (step, LANES), 0) // 2)

    def shift(scratch, beam, row, value):
        value = pltpu.roll(value, places[beam][1], 1)
        scratch[beam, row : row + step, :] = value
        scratch[beam, rows + row : rows + row + step, :] = value

    def total(scratch, row):
        inside = outside = 0.0
        for beam in range(beams):
            tile, rest_px = places[beam]
            base = rows + row - 2 * tile
            here = scratch[beam, pl.ds(base, step), :]
            before = scratch[beam, pl.ds(base - 2, step), :]
            part = jnp.where(lane >= rest_px, here, before)
            own_pixel = pixel >= offsets_ref[beam] - row // 2 * LANES
            inside = inside + jnp.where(own_pixel, part, 0.0)
            outside = outside + jnp.where(own_pixel, 0.0, part)
        return inside, outside

    @pl.when(pl.program_id(0) == 0)
    def _():
        for beam in range(beams):
            for row in range(0, rows, step):
                shift(shifted[0], beam, row, weights_ref[beam, row : row + step, :])
        for row in range(0, rows, step):
            for wsum_ref, value in zip(wsum_refs, total(shifted[0], row)):
                wsum_ref[row : row + step, :] = value

    def emit(channel, row):
        inside, outside = total(shifted[channel], row)
        for index in range(0, step // share, 2):
            chip = (row // share + index) // 2
            cut = [slice(part * share, (part + 1) * share) for part in (index, index + 1)]
            for side, value in enumerate((inside, outside)):
                same = jnp.where(first_core, value[cut[0]], value[cut[1]])
                other = jnp.where(first_core, value[cut[1]], value[cut[0]])
                if side == 0:
                    own[0][chip, channel], own[1][chip, channel] = same, other
                    continue
                for part, (begin, count) in enumerate(spans):
                    keep[part][chip, channel] = same[begin : begin + count]
                    give[part][chip, channel] = other[begin : begin + count]

    for channel in range(block + 1):
        for row in range(0, rows, step):
            if channel < block:
                for beam in range(beams):
                    weight = weights_ref[beam, row : row + step, :]
                    value = images_ref[beam, channel, row : row + step, :]
                    shift(shifted[channel], beam, row, value * weight)
            if channel:
                emit(channel - 1, row)


def channel_block(channels):
    return max(size for size in range(1, 7) if channels % size == 0)


def gather(chips, spans, starts, me, weights, images):
    beams, channels, rows, _ = images.shape
    block = channel_block(channels)
    chunks = len(spans)
    counts = [rows // (2 * chips)] * 2 + [count for _, count in spans] * 2
    result = pl.pallas_call(
        functools.partial(gather_kernel, spans),
        grid_spec=pltpu.PrefetchScalarGridSpec(
            num_scalar_prefetch=2,
            grid=(channels // block,),
            in_specs=[
                pl.BlockSpec((beams, rows, LANES), lambda step, *_: (0, 0, 0)),
                pl.BlockSpec((beams, block, rows, LANES), lambda step, *_: (0, step, 0, 0)),
            ],
            out_specs=[
                pl.BlockSpec((chips, block, count, LANES), lambda step, *_: (0, step, 0, 0))
                for count in counts
            ]
            + [pl.BlockSpec((rows, LANES), lambda step, *_: (0, 0))] * 2,
            scratch_shapes=[pltpu.VMEM((beams, 2 * rows, LANES), jnp.float32)] * block,
        ),
        out_shape=[
            jax.ShapeDtypeStruct((chips, channels, count, LANES), jnp.float32) for count in counts
        ]
        + [jax.ShapeDtypeStruct((rows, LANES), jnp.float32)] * 2,
        compiler_params=pltpu.CompilerParams(vmem_limit_bytes=VMEM),
        name="gather",
    )(starts, me, weights, images)
    return result[:2], result[2 : 2 + chunks], result[2 + chunks : 2 + 2 * chunks], result[-2:]


def combine_kernel(first, me_ref, scale_ref, *refs):
    own, arrived, outs = refs[:2], refs[2:4], refs[4:]
    count = outs[0].shape[2]
    rows = slice(first, first + count)
    for index, out in enumerate(outs):
        chip = jnp.bitwise_xor(lax.div(me_ref[0], 2), index)
        scale = 1.0 / scale_ref[chip, rows, :]
        for side in range(2):
            total = own[side][chip, :, rows, :] + arrived[side][chip]
            out[side] = total * scale[None]


def combine(begin, me, scale, own, arrived):
    chips, channels, _, _ = own[0].shape
    count = arrived[0].shape[2]
    tall = max(8, count)
    block = channels // 3
    wide = pl.BlockSpec((chips, block, tall, LANES), lambda step, _: (0, step, begin // tall, 0))
    part = pl.BlockSpec((chips, block, count, LANES), lambda step, _: (0, step, 0, 0))
    return pl.pallas_call(
        functools.partial(combine_kernel, begin % tall),
        grid_spec=pltpu.PrefetchScalarGridSpec(
            num_scalar_prefetch=1,
            grid=(3,),
            in_specs=[pl.BlockSpec((chips, tall, LANES), lambda step, _: (0, begin // tall, 0))]
            + [wide] * 2
            + [part] * 2,
            out_specs=[pl.BlockSpec((2, block, count, LANES), lambda step, _: (0, step, 0, 0))]
            * chips,
        ),
        out_shape=[jax.ShapeDtypeStruct((2, channels, count, LANES), jnp.float32)] * chips,
        compiler_params=pltpu.CompilerParams(vmem_limit_bytes=VMEM),
        name="combine",
    )(me, scale, *own, *arrived)


def scatter_kernel(spans, aliased, offsets_ref, weights_ref, *rest):
    chunks = len(spans)
    if aliased:
        rest = rest[1:]
    own, following = rest[:chunks], rest[chunks : 2 * chunks]
    out_ref, joined = rest[2 * chunks], rest[2 * chunks + 1 :]
    beams, block, rows, _ = out_ref.shape
    members = own[0].shape[0]
    share = rows // members
    step = 64
    lane = lax.broadcasted_iota(jnp.int32, (step, LANES), 1)
    places = [place(offsets_ref, beam) for beam in range(beams)]
    for channel in range(block):
        for half, pieces in enumerate((own, following)):
            for member in range(members):
                for piece, (begin, count) in zip(pieces, spans):
                    row = half * rows + member * share + begin
                    joined[channel][row : row + count, :] = piece[member, channel]
        for beam in range(beams):
            tile, rest_px = places[beam]
            for row in range(0, rows, step):
                base = 2 * tile + row
                here = joined[channel][pl.ds(base, step), :]
                after = joined[channel][pl.ds(base + 2, step), :]
                value = jnp.where(lane >= rest_px, here, after)
                value = pltpu.roll(value, lax.rem(LANES - rest_px, LANES), 1)
                out_ref[beam, channel, row : row + step, :] = (
                    value * weights_ref[beam, row : row + step, :]
                )


def scatter(spans, first, width, starts, weights, own, following, output):
    beams, rows, _ = weights.shape
    members, channels, _, _ = own[0].shape
    block = max(size for size in range(1, 10) if width % size == 0)
    aliased = output is not None

    def piece(array, count):
        base = first // block if array.shape[1] == channels else 0
        shape = (members, block, count, LANES)
        return pl.BlockSpec(shape, lambda step, _: (0, base + step, 0, 0))

    return pl.pallas_call(
        functools.partial(scatter_kernel, spans, aliased),
        grid_spec=pltpu.PrefetchScalarGridSpec(
            num_scalar_prefetch=1,
            grid=(width // block,),
            in_specs=[pl.BlockSpec((beams, rows, LANES), lambda step, _: (0, 0, 0))]
            + [pl.BlockSpec(memory_space=pl.ANY)] * aliased
            + [piece(array, count) for part in (own, following) for array, (_, count) in zip(part, spans)],
            out_specs=pl.BlockSpec(
                (beams, block, rows, LANES), lambda step, _: (0, first // block + step, 0, 0)
            ),
            scratch_shapes=[pltpu.VMEM((2 * rows, LANES), jnp.float32)] * block,
        ),
        out_shape=jax.ShapeDtypeStruct((beams, channels, rows, LANES), jnp.float32),
        input_output_aliases={2: 0} if aliased else {},
        compiler_params=pltpu.CompilerParams(vmem_limit_bytes=VMEM),
        name="scatter",
    )(starts, weights, *([output] if aliased else []), *own, *following)


def split(value):
    high = value.astype(jnp.bfloat16)
    return high, (value - high.astype(jnp.float32)).astype(jnp.bfloat16)


def deconvolve_kernel(aliased, groups, chips, me_ref, *refs):
    flat_refs, refs = refs[:chips], refs[chips:]
    if aliased:
        refs = refs[:2] + refs[3:]
    synth_ref, forward_ref, resid_ref, model_ref = refs[:4]
    refs = (None, *refs)
    flat, resid, x, y, product, field = (
        refs[5 + kind * groups : 5 + (kind + 1) * groups] for kind in range(6)
    )
    level = refs[5 + 6 * groups]
    channels = flat[0].shape[0]
    half = field[0].shape[1]
    pixels = field[0].shape[2]
    tiles = pixels // LANES
    stride = 2 * groups * tiles
    sub = 16
    left, right = slice(0, pixels), slice(pixels, 2 * pixels)
    last = lax.broadcasted_iota(jnp.int32, (sub, pixels), 0) == sub - 1

    places = [
        (tile, q, slice(q * pixels + tile * LANES, q * pixels + (tile + 1) * LANES))
        for tile in range(tiles)
        for q in range(2)
    ]

    def feed(group, row, value):
        high, low = split(value)
        for part, piece in enumerate((high, low, high)):
            x[group][part * channels + row : part * channels + row + sub, :] = piece

    def load(group):
        for tile, q, lanes in places:
            size = channels // chips
            for chip, ref in enumerate(flat_refs):
                flat[group][chip * size : (chip + 1) * size, lanes] = ref[
                    pl.ds(2 * (group * tiles + tile) + q, size, stride=stride), :
                ]
        for row in range(0, channels, sub):
            feed(group, row, flat[group][row : row + sub, :])
        extra = x[group].shape[0] - 3 * channels
        x[group][3 * channels :, :] = jnp.zeros((extra, 2 * pixels), jnp.bfloat16)

    def synthesize(group):
        product[group][...] = jnp.dot(
            synth_ref[...], x[group][...], preferred_element_type=jnp.float32
        )

    def project(group):
        resid[group][...] = jnp.dot(
            forward_ref[:, : 4 * half], y[group][...], preferred_element_type=jnp.float32
        ) + jnp.dot(
            forward_ref[:, 4 * half :], y[group][: 2 * half, :], preferred_element_type=jnp.float32
        )

    def step_of(group, row, old):
        rows, low_rows = slice(row, row + sub), slice(half + row, half + row + sub)
        cos_q, cos_u = product[group][rows, left], product[group][rows, right]
        sin_q, sin_u = product[group][low_rows, left], product[group][low_rows, right]
        real_p, real_n = cos_q + sin_u, cos_q - sin_u
        imag_p, imag_n = cos_u - sin_q, cos_u + sin_q
        if row + sub == half:
            real_p = jnp.where(last, product[group][2 * half : 2 * half + 1, left], real_p)
            imag_p = jnp.where(last, product[group][2 * half : 2 * half + 1, right], imag_p)
        values = [real_p, real_n, imag_p, imag_n]
        if old:
            values = [value + field[group][part, rows, :] for part, value in enumerate(values)]
        real_p, real_n, imag_p, imag_n = values
        return values, real_p * real_p + imag_p * imag_p, real_n * real_n + imag_n * imag_n

    def shrink(group, old):
        if not old:
            largest = jnp.zeros((sub, pixels), jnp.float32)
            for row in range(0, half, sub):
                _, power_p, power_n = step_of(group, row, old)
                largest = jnp.maximum(largest, jnp.maximum(power_p, power_n))
            top = jnp.sqrt(jnp.max(largest, axis=0, keepdims=True))
            level[group] = jnp.broadcast_to(
                THRESH_FRAC / STEP_GAIN * top + THRESH_BASE, level.shape[1:]
            )
        limit = level[group]
        for row in range(0, half, sub):
            rows = slice(row, row + sub)
            values, power_p, power_n = step_of(group, row, old)
            factor_p = jnp.maximum(1.0 - limit * lax.rsqrt(power_p), 0.0)
            factor_n = jnp.maximum(1.0 - limit * lax.rsqrt(power_n), 0.0)
            values = [
                value * factor for value, factor in zip(values, (factor_p, factor_n) * 2)
            ]
            for part, value in enumerate(values):
                field[group][part, rows, :] = value
            real_p, real_n, imag_p, imag_n = values
            if row + sub == half:
                real_p, imag_p = jnp.where(last, 0.0, real_p), jnp.where(last, 0.0, imag_p)
            for base, lanes, value in (
                (0, left, real_p + real_n),
                (0, right, imag_p + imag_n),
                (half, left, imag_n - imag_p),
                (half, right, real_p - real_n),
            ):
                high, low = split(value)
                y[group][base + row : base + row + sub, lanes] = high
                y[group][2 * half + base + row : 2 * half + base + row + sub, lanes] = low

    def subtract(group):
        middle = jnp.concatenate(
            [field[group][0, half - 1 : half, :], field[group][2, half - 1 : half, :]], 1
        )
        for row in range(0, channels, sub):
            rows = slice(row, row + sub)
            value = flat[group][rows, :] - (resid[group][rows, :] + middle)
            resid[group][rows, :] = value
            feed(group, row, value)

    def iterate(old):
        for group in range(groups):
            shrink(group, old)
            if group + 1 < groups:
                synthesize(group + 1)
            else:
                project(0)
        for group in range(groups):
            subtract(group)
            if group + 1 < groups:
                project(group + 1)
            else:
                synthesize(0)

    for group in range(groups):
        load(group)
    synthesize(0)
    iterate(False)

    def repeat(number, carry):
        iterate(True)
        return carry

    lax.fori_loop(1, ITERS, repeat, 0)

    for group in range(groups):
        for tile, q, side in places:
            size = channels // (2 * chips)
            for part in range(2 * chips):
                base = jnp.bitwise_xor(me_ref[0], part) * (size * stride)
                base = base + (2 * (group * tiles + tile) + q)
                resid_ref[pl.ds(base, size, stride=stride), :] = resid[group][
                    part * size : (part + 1) * size, side
                ]
        lanes = slice(group * pixels, (group + 1) * pixels)
        for part in range(2):
            model_ref[part, half : half + 1, lanes] = field[group][2 * part, half - 1 : half, :]
            model_ref[part, half + 1 :, lanes] = field[group][2 * part, : half - 1, :]

    turn = 32

    def reverse(index, carry):
        row = pl.multiple_of(index * turn, turn)
        for part in range(2):
            value = jnp.concatenate(
                [field[group][2 * part + 1, pl.ds(row, turn), :] for group in range(groups)], 1
            )
            for line in range(turn):
                model_ref[part, pl.ds(half - 1 - line - row, 1), :] = value[line : line + 1, :]
        return carry

    lax.fori_loop(0, half // turn, reverse, 0)


def deconvolve(begin, depths, pixels, me, cube, synth, forward, model):
    chips = len(cube)
    _, group, rows, _ = cube[0].shape
    channels = 2 * chips * group
    half = depths // 2
    size = rows // 2 * LANES
    groups = max(1, size // GROUP)
    wide = size // groups
    cube = [part.reshape(-1, LANES) for part in cube]
    whole = (channels * rows, LANES)
    aliased = model is not None
    resid, model = pl.pallas_call(
        functools.partial(deconvolve_kernel, aliased, groups, chips),
        grid_spec=pltpu.PrefetchScalarGridSpec(
            num_scalar_prefetch=1,
            grid=(1,),
            in_specs=[pl.BlockSpec(part.shape, lambda step, _: (0, 0)) for part in cube]
            + [
                pl.BlockSpec(synth.shape, lambda step, _: (0, 0)),
                pl.BlockSpec(forward.shape, lambda step, _: (0, 0)),
            ]
            + [pl.BlockSpec(memory_space=pl.ANY)] * aliased,
            out_specs=[
                pl.BlockSpec(whole, lambda step, _: (0, 0)),
                pl.BlockSpec((2, depths, size), lambda step, _: (0, 0, begin // rows)),
            ],
            scratch_shapes=[pltpu.VMEM((channels, 2 * wide), jnp.float32)] * (2 * groups)
            + [pltpu.VMEM((synth.shape[1], 2 * wide), jnp.bfloat16)] * groups
            + [pltpu.VMEM((4 * half, 2 * wide), jnp.bfloat16)] * groups
            + [pltpu.VMEM((synth.shape[0], 2 * wide), jnp.float32)] * groups
            + [pltpu.VMEM((4, half, wide), jnp.float32)] * groups
            + [pltpu.VMEM((groups, 16, wide), jnp.float32)],
        ),
        out_shape=[
            jax.ShapeDtypeStruct(whole, jnp.float32),
            jax.ShapeDtypeStruct((2, depths, pixels), jnp.float32),
        ],
        input_output_aliases={3 + chips: 1} if aliased else {},
        compiler_params=pltpu.CompilerParams(vmem_limit_bytes=VMEM),
        name="deconvolve",
    )(me, *cube, synth, forward, *([model] if aliased else []))
    return resid.reshape(2 * chips, group, rows, LANES), model


def chunk_spans(share):
    if share % 8:
        return ((0, share),)
    return tuple((row, 8) for row in range(0, share, 8))


def body(depths, *arrays):
    return run(depths, *arrays)


def run(depths, beam_images, beam_weights, offsets):
    beams, _, group, tile = beam_images.shape
    members = lax.axis_size("chan")
    sky = lax.axis_size("sky")
    pixels = tile // members
    lines = tile // LANES
    share = 2 * lines // members
    spans = chunk_spans(share)
    channels = group * members
    starts = offsets - lax.axis_index("sky") * tile
    images = beam_images.reshape(beams, 2, group, lines, LANES).transpose(0, 2, 3, 1, 4)
    images = images.reshape(beams, group, 2 * lines, LANES)
    weights = jnp.repeat(beam_weights.reshape(beams, lines, LANES), 2, axis=1)
    chips = members // 2
    me = lax.axis_index("chan").astype(jnp.int32)
    mine = me.reshape(1)
    ahead = [
        [(t * members + c, (t + 1) * members + (c ^ other)) for t in range(sky - 1) for c in range(members)]
        for other in range(2)
    ]
    backward_pairs = [(index + 1, index) for index in range(sky - 1)]
    both = ("sky", "chan")

    own, keep, give, weight = gather(chips, spans, starts, mine, weights, images)
    arrived = []
    for chunk in range(len(spans)):
        straight = lax.ppermute(keep[chunk], both, ahead[0])
        arrived.append((straight, lax.ppermute(give[chunk], both, ahead[1])))
    crossed = lax.ppermute(own[1], "chan", [(c, c ^ 1) for c in range(members)])
    arrived_w = lax.ppermute(weight[1], both, ahead[0])
    scale = (weight[0] + arrived_w + COMBINE_FLOOR).reshape(chips, 2, share, LANES)
    scale = lax.dynamic_index_in_dim(scale, lax.rem(me, 2), 1, keepdims=False)
    order = jnp.bitwise_xor(me, jnp.arange(members, dtype=jnp.int32))
    synth, forward = depth_tables(channels, depths, order)

    model = None
    resid, following = [], []
    for chunk, (begin, count) in enumerate(spans):
        cube = list(combine(begin, mine, scale, (own[0], crossed), arrived[chunk]))
        for index in range(1, chips):
            pairs = [(c, c ^ (2 * index)) for c in range(members)]
            cube[index] = lax.ppermute(cube[index], "chan", pairs)
        part, model = deconvolve(begin, depths, pixels, mine, cube, synth, forward, model)
        part = lax.all_to_all(part, "chan", 0, 0, tiled=True)
        resid.append(part)
        if chunk + 1 < len(spans):
            following.append(lax.ppermute(part, "sky", backward_pairs))
    parts = 2 if group % 2 == 0 else 1
    width = group // parts
    late = []
    for index in range(parts):
        late.append(lax.ppermute(part[:, index * width : (index + 1) * width], "sky", backward_pairs))
    outputs = None
    for index in range(parts):
        outputs = scatter(
            spans, index * width, width, starts, weights, resid, [*following, late[index]], outputs
        )
    outputs = outputs.reshape(beams, group, lines, 2, LANES).transpose(0, 3, 1, 2, 4)
    return outputs.reshape(beam_images.shape), model


DEPTHS = 512


def solution(mesh):
    in_specs = (P("sky", None, "chan", None), P("sky", None), P("sky"))
    out_specs = (P("sky", None, "chan", None), P(None, None, ("sky", "chan")))
    return jax.shard_map(
        functools.partial(body, DEPTHS),
        mesh=mesh,
        in_specs=in_specs,
        out_specs=out_specs,
        check_vma=False,
    )
```

```python
import functools

import jax
import jax.numpy as jnp
from jax import lax
from jax.experimental import pallas as pl
from jax.experimental.pallas import tpu as pltpu
from jax.sharding import PartitionSpec as P


ITERS = 3

BAND_LOW = 800000000.0
BAND_WIDTH = 288000000.0
LIGHT = 299792458.0
DEPTH_STEP = 20.0
COMBINE_FLOOR = 0.5
THRESH_FRAC = 0.25
THRESH_BASE = 0.005
STEP_GAIN = 0.5

LANES = 128
GROUP = 128
VMEM = 67043328


def split_rows(arrays):
    high = lax.reduce_precision(arrays, 8, 7)
    return high.astype(jnp.bfloat16), (arrays - high).astype(jnp.bfloat16)


def depth_tables(channels, depths, order):
    half = depths // 2
    channel = jnp.arange(channels, dtype=jnp.float32)
    freq = BAND_LOW + (channel + 0.5) * (BAND_WIDTH / channels)
    lam_sq = (LIGHT / freq) ** 2
    lam_sq = lam_sq - jnp.mean(lam_sq)
    lam_sq = lam_sq.reshape(order.shape[0], -1)[order].reshape(-1)
    depth = (jnp.arange(half, dtype=jnp.float32) + 1.0) * DEPTH_STEP
    angle = 2.0 * depth[:, None] * lam_sq[None, :]
    cosine = jnp.cos(angle)
    sine = jnp.sin(angle)
    ones = jnp.concatenate([jnp.ones((1, channels)), jnp.zeros((15, channels))], 0)
    synth = jnp.concatenate([cosine, sine, ones], 0) / channels * STEP_GAIN
    high, low = split_rows(synth)
    pad = -3 * channels % LANES
    synth = jnp.concatenate([high, high, low, jnp.zeros((high.shape[0], pad), jnp.bfloat16)], 1)
    forward = jnp.concatenate([cosine, sine], 0).T
    high, low = split_rows(forward)
    return synth, jnp.concatenate([high, high, low], 1)


def place(offsets_ref, beam):
    start = offsets_ref[beam]
    return lax.div(start, LANES), lax.rem(start, LANES)


def gather_kernel(spans, offsets_ref, me_ref, weights_ref, images_ref, *rest):
    chunks = len(spans)
    own, keep, give = rest[:2], rest[2 : 2 + chunks], rest[2 + chunks : 2 + 2 * chunks]
    wsum_refs, shifted = rest[2 + 2 * chunks : 4 + 2 * chunks], rest[4 + 2 * chunks :]
    first_core = lax.rem(me_ref[0], 2) == 0
    beams, block, rows, _ = images_ref.shape
    share = own[0].shape[2]
    step = max(64, 2 * share)
    lane = lax.broadcasted_iota(jnp.int32, (step, LANES), 1)
    places = [place(offsets_ref, beam) for beam in range(beams)]

    pixel = lane + LANES * (lax.broadcasted_iota(jnp.int32, (step, LANES), 0) // 2)

    def shift(scratch, beam, row, value):
        value = pltpu.roll(value, places[beam][1], 1)
        scratch[beam, row : row + step, :] = value
        scratch[beam, rows + row : rows + row + step, :] = value

    def total(scratch, row):
        inside = outside = 0.0
        for beam in range(beams):
            tile, rest_px = places[beam]
            base = rows + row - 2 * tile
            here = scratch[beam, pl.ds(base, step), :]
            before = scratch[beam, pl.ds(base - 2, step), :]
            part = jnp.where(lane >= rest_px, here, before)
            own_pixel = pixel >= offsets_ref[beam] - row // 2 * LANES
            inside = inside + jnp.where(own_pixel, part, 0.0)
            outside = outside + jnp.where(own_pixel, 0.0, part)
        return inside, outside

    @pl.when(pl.program_id(0) == 0)
    def _():
        for beam in range(beams):
            for row in range(0, rows, step):
                shift(shifted[0], beam, row, weights_ref[beam, row : row + step, :])
        for row in range(0, rows, step):
            for wsum_ref, value in zip(wsum_refs, total(shifted[0], row)):
                wsum_ref[row : row + step, :] = value

    def emit(channel, row):
        inside, outside = total(shifted[channel], row)
        for index in range(0, step // share, 2):
            chip = (row // share + index) // 2
            cut = [slice(part * share, (part + 1) * share) for part in (index, index + 1)]
            for side, value in enumerate((inside, outside)):
                same = jnp.where(first_core, value[cut[0]], value[cut[1]])
                other = jnp.where(first_core, value[cut[1]], value[cut[0]])
                if side == 0:
                    own[0][chip, channel], own[1][chip, channel] = same, other
                    continue
                for part, (begin, count) in enumerate(spans):
                    keep[part][chip, channel] = same[begin : begin + count]
                    give[part][chip, channel] = other[begin : begin + count]

    for channel in range(block + 1):
        for row in range(0, rows, step):
            if channel < block:
                for beam in range(beams):
                    weight = weights_ref[beam, row : row + step, :]
                    value = images_ref[beam, channel, row : row + step, :]
                    shift(shifted[channel], beam, row, value * weight)
            if channel:
                emit(channel - 1, row)


def channel_block(channels):
    return max(size for size in range(1, 7) if channels % size == 0)


def gather(chips, spans, starts, me, weights, images):
    beams, channels, rows, _ = images.shape
    block = channel_block(channels)
    chunks = len(spans)
    counts = [rows // (2 * chips)] * 2 + [count for _, count in spans] * 2
    result = pl.pallas_call(
        functools.partial(gather_kernel, spans),
        grid_spec=pltpu.PrefetchScalarGridSpec(
            num_scalar_prefetch=2,
            grid=(channels // block,),
            in_specs=[
                pl.BlockSpec((beams, rows, LANES), lambda step, *_: (0, 0, 0)),
                pl.BlockSpec((beams, block, rows, LANES), lambda step, *_: (0, step, 0, 0)),
            ],
            out_specs=[
                pl.BlockSpec((chips, block, count, LANES), lambda step, *_: (0, step, 0, 0))
                for count in counts
            ]
            + [pl.BlockSpec((rows, LANES), lambda step, *_: (0, 0))] * 2,
            scratch_shapes=[pltpu.VMEM((beams, 2 * rows, LANES), jnp.float32)] * block,
        ),
        out_shape=[
            jax.ShapeDtypeStruct((chips, channels, count, LANES), jnp.float32) for count in counts
        ]
        + [jax.ShapeDtypeStruct((rows, LANES), jnp.float32)] * 2,
        compiler_params=pltpu.CompilerParams(vmem_limit_bytes=VMEM),
        name="gather",
    )(starts, me, weights, images)
    return result[:2], result[2 : 2 + chunks], result[2 + chunks : 2 + 2 * chunks], result[-2:]


def combine_kernel(first, me_ref, scale_ref, *refs):
    own, arrived, outs = refs[:2], refs[2:4], refs[4:]
    count = outs[0].shape[2]
    rows = slice(first, first + count)
    for index, out in enumerate(outs):
        chip = jnp.bitwise_xor(lax.div(me_ref[0], 2), index)
        scale = 1.0 / scale_ref[chip, rows, :]
        for side in range(2):
            total = own[side][chip, :, rows, :] + arrived[side][chip]
            out[side] = total * scale[None]


def combine(begin, me, scale, own, arrived):
    chips, channels, _, _ = own[0].shape
    count = arrived[0].shape[2]
    tall = max(8, count)
    block = channels // 3
    wide = pl.BlockSpec((chips, block, tall, LANES), lambda step, _: (0, step, begin // tall, 0))
    part = pl.BlockSpec((chips, block, count, LANES), lambda step, _: (0, step, 0, 0))
    return pl.pallas_call(
        functools.partial(combine_kernel, begin % tall),
        grid_spec=pltpu.PrefetchScalarGridSpec(
            num_scalar_prefetch=1,
            grid=(3,),
            in_specs=[pl.BlockSpec((chips, tall, LANES), lambda step, _: (0, begin // tall, 0))]
            + [wide] * 2
            + [part] * 2,
            out_specs=[pl.BlockSpec((2, block, count, LANES), lambda step, _: (0, step, 0, 0))]
            * chips,
        ),
        out_shape=[jax.ShapeDtypeStruct((2, channels, count, LANES), jnp.float32)] * chips,
        compiler_params=pltpu.CompilerParams(vmem_limit_bytes=VMEM),
        name="combine",
    )(me, scale, *own, *arrived)


def scatter_kernel(spans, aliased, offsets_ref, weights_ref, *rest):
    chunks = len(spans)
    if aliased:
        rest = rest[1:]
    own, following = rest[:chunks], rest[chunks : 2 * chunks]
    out_ref, joined = rest[2 * chunks], rest[2 * chunks + 1 :]
    beams, block, rows, _ = out_ref.shape
    members = own[0].shape[0]
    share = rows // members
    step = 64
    lane = lax.broadcasted_iota(jnp.int32, (step, LANES), 1)
    places = [place(offsets_ref, beam) for beam in range(beams)]
    batch = len(joined)

    def write(turn, carry):
        for slot, scratch in enumerate(joined):
            channel = turn * batch + slot
            for half, pieces in enumerate((own, following)):
                for member in range(members):
                    for piece, (begin, count) in zip(pieces, spans):
                        row = half * rows + member * share + begin
                        scratch[row : row + count, :] = piece[member, channel]
            for beam in range(beams):
                tile, rest_px = places[beam]
                for row in range(0, rows, step):
                    base = 2 * tile + row
                    here = scratch[pl.ds(base, step), :]
                    after = scratch[pl.ds(base + 2, step), :]
                    value = jnp.where(lane >= rest_px, here, after)
                    value = pltpu.roll(value, lax.rem(LANES - rest_px, LANES), 1)
                    out_ref[beam, channel, row : row + step, :] = (
                        value * weights_ref[beam, row : row + step, :]
                    )
        return carry

    lax.fori_loop(0, block // batch, write, 0)


def scatter(spans, first, width, starts, weights, own, following, output):
    beams, rows, _ = weights.shape
    members, channels, _, _ = own[0].shape
    block = max(size for size in range(3, 10, 3) if width % size == 0)
    aliased = output is not None

    def piece(array, count):
        base = first // block if array.shape[1] == channels else 0
        shape = (members, block, count, LANES)
        return pl.BlockSpec(shape, lambda step, _: (0, base + step, 0, 0))

    return pl.pallas_call(
        functools.partial(scatter_kernel, spans, aliased),
        grid_spec=pltpu.PrefetchScalarGridSpec(
            num_scalar_prefetch=1,
            grid=(width // block,),
            in_specs=[pl.BlockSpec((beams, rows, LANES), lambda step, _: (0, 0, 0))]
            + [pl.BlockSpec(memory_space=pl.ANY)] * aliased
            + [piece(array, count) for part in (own, following) for array, (_, count) in zip(part, spans)],
            out_specs=pl.BlockSpec(
                (beams, block, rows, LANES), lambda step, _: (0, first // block + step, 0, 0)
            ),
            scratch_shapes=[pltpu.VMEM((2 * rows, LANES), jnp.float32)] * 1,
        ),
        out_shape=jax.ShapeDtypeStruct((beams, channels, rows, LANES), jnp.float32),
        input_output_aliases={2: 0} if aliased else {},
        compiler_params=pltpu.CompilerParams(vmem_limit_bytes=VMEM),
        name="scatter",
    )(starts, weights, *([output] if aliased else []), *own, *following)


def split(value):
    high = value.astype(jnp.bfloat16)
    return high, (value - high.astype(jnp.float32)).astype(jnp.bfloat16)


def deconvolve_kernel(aliased, groups, chips, me_ref, *refs):
    flat_refs, refs = refs[:chips], refs[chips:]
    if aliased:
        refs = refs[:2] + refs[3:]
    synth_ref, forward_ref, resid_ref, model_ref = refs[:4]
    refs = (None, *refs)
    flat, resid, x, y, product, field = (
        refs[5 + kind * groups : 5 + (kind + 1) * groups] for kind in range(6)
    )
    level = refs[5 + 6 * groups]
    channels = flat[0].shape[0]
    half = field[0].shape[1]
    pixels = field[0].shape[2]
    tiles = pixels // LANES
    stride = 2 * groups * tiles
    sub = 16
    left, right = slice(0, pixels), slice(pixels, 2 * pixels)
    last = lax.broadcasted_iota(jnp.int32, (sub, pixels), 0) == sub - 1

    places = [
        (tile, q, slice(q * pixels + tile * LANES, q * pixels + (tile + 1) * LANES))
        for tile in range(tiles)
        for q in range(2)
    ]

    def feed(group, row, value):
        high, low = split(value)
        for part, piece in enumerate((high, low, high)):
            x[group][part * channels + row : part * channels + row + sub, :] = piece

    def load(group):
        for tile, q, lanes in places:
            size = channels // chips
            for chip, ref in enumerate(flat_refs):
                flat[group][chip * size : (chip + 1) * size, lanes] = ref[
                    pl.ds(2 * (group * tiles + tile) + q, size, stride=stride), :
                ]
        for row in range(0, channels, sub):
            feed(group, row, flat[group][row : row + sub, :])
        extra = x[group].shape[0] - 3 * channels
        x[group][3 * channels :, :] = jnp.zeros((extra, 2 * pixels), jnp.bfloat16)

    def synthesize(group):
        product[group][...] = jnp.dot(
            synth_ref[...], x[group][...], preferred_element_type=jnp.float32
        )

    def project(group):
        resid[group][...] = jnp.dot(
            forward_ref[:, : 4 * half], y[group][...], preferred_element_type=jnp.float32
        ) + jnp.dot(
            forward_ref[:, 4 * half :], y[group][: 2 * half, :], preferred_element_type=jnp.float32
        )

    def step_of(group, row, old):
        rows, low_rows = slice(row, row + sub), slice(half + row, half + row + sub)
        cos_q, cos_u = product[group][rows, left], product[group][rows, right]
        sin_q, sin_u = product[group][low_rows, left], product[group][low_rows, right]
        real_p, real_n = cos_q + sin_u, cos_q - sin_u
        imag_p, imag_n = cos_u - sin_q, cos_u + sin_q
        if row + sub == half:
            real_p = jnp.where(last, product[group][2 * half : 2 * half + 1, left], real_p)
            imag_p = jnp.where(last, product[group][2 * half : 2 * half + 1, right], imag_p)
        values = [real_p, real_n, imag_p, imag_n]
        if old:
            values = [value + field[group][part, rows, :] for part, value in enumerate(values)]
        real_p, real_n, imag_p, imag_n = values
        return values, real_p * real_p + imag_p * imag_p, real_n * real_n + imag_n * imag_n

    def shrink(group, old):
        if not old:
            largest = jnp.zeros((sub, pixels), jnp.float32)
            for row in range(0, half, sub):
                _, power_p, power_n = step_of(group, row, old)
                largest = jnp.maximum(largest, jnp.maximum(power_p, power_n))
            top = jnp.sqrt(jnp.max(largest, axis=0, keepdims=True))
            level[group] = jnp.broadcast_to(
                THRESH_FRAC / STEP_GAIN * top + THRESH_BASE, level.shape[1:]
            )
        limit = level[group]
        for row in range(0, half, sub):
            rows = slice(row, row + sub)
            values, power_p, power_n = step_of(group, row, old)
            factor_p = jnp.maximum(1.0 - limit * lax.rsqrt(power_p), 0.0)
            factor_n = jnp.maximum(1.0 - limit * lax.rsqrt(power_n), 0.0)
            values = [
                value * factor for value, factor in zip(values, (factor_p, factor_n) * 2)
            ]
            for part, value in enumerate(values):
                field[group][part, rows, :] = value
            real_p, real_n, imag_p, imag_n = values
            if row + sub == half:
                real_p, imag_p = jnp.where(last, 0.0, real_p), jnp.where(last, 0.0, imag_p)
            for base, lanes, value in (
                (0, left, real_p + real_n),
                (0, right, imag_p + imag_n),
                (half, left, imag_n - imag_p),
                (half, right, real_p - real_n),
            ):
                high, low = split(value)
                y[group][base + row : base + row + sub, lanes] = high
                y[group][2 * half + base + row : 2 * half + base + row + sub, lanes] = low

    def subtract(group):
        middle = jnp.concatenate(
            [field[group][0, half - 1 : half, :], field[group][2, half - 1 : half, :]], 1
        )
        for row in range(0, channels, sub):
            rows = slice(row, row + sub)
            value = flat[group][rows, :] - (resid[group][rows, :] + middle)
            resid[group][rows, :] = value
            feed(group, row, value)

    def iterate(old):
        for group in range(groups):
            shrink(group, old)
            if group + 1 < groups:
                synthesize(group + 1)
            else:
                project(0)
        for group in range(groups):
            subtract(group)
            if group + 1 < groups:
                project(group + 1)
            else:
                synthesize(0)

    for group in range(groups):
        load(group)
    synthesize(0)
    iterate(False)

    def repeat(number, carry):
        iterate(True)
        return carry

    lax.fori_loop(1, ITERS, repeat, 0)

    for group in range(groups):
        for tile, q, side in places:
            size = channels // (2 * chips)
            for part in range(2 * chips):
                base = jnp.bitwise_xor(me_ref[0], part) * (size * stride)
                base = base + (2 * (group * tiles + tile) + q)
                resid_ref[pl.ds(base, size, stride=stride), :] = resid[group][
                    part * size : (part + 1) * size, side
                ]
        lanes = slice(group * pixels, (group + 1) * pixels)
        for part in range(2):
            model_ref[part, half : half + 1, lanes] = field[group][2 * part, half - 1 : half, :]
            model_ref[part, half + 1 :, lanes] = field[group][2 * part, : half - 1, :]

    turn = 32

    def reverse(index, carry):
        row = pl.multiple_of(index * turn, turn)
        for part in range(2):
            value = jnp.concatenate(
                [field[group][2 * part + 1, pl.ds(row, turn), :] for group in range(groups)], 1
            )
            for line in range(turn):
                model_ref[part, pl.ds(half - 1 - line - row, 1), :] = value[line : line + 1, :]
        return carry

    lax.fori_loop(0, half // turn, reverse, 0)


def deconvolve(begin, depths, pixels, me, cube, synth, forward, model):
    chips = len(cube)
    _, group, rows, _ = cube[0].shape
    channels = 2 * chips * group
    half = depths // 2
    size = rows // 2 * LANES
    groups = max(1, size // GROUP)
    wide = size // groups
    cube = [part.reshape(-1, LANES) for part in cube]
    whole = (channels * rows, LANES)
    aliased = model is not None
    resid, model = pl.pallas_call(
        functools.partial(deconvolve_kernel, aliased, groups, chips),
        grid_spec=pltpu.PrefetchScalarGridSpec(
            num_scalar_prefetch=1,
            grid=(1,),
            in_specs=[pl.BlockSpec(part.shape, lambda step, _: (0, 0)) for part in cube]
            + [
                pl.BlockSpec(synth.shape, lambda step, _: (0, 0)),
                pl.BlockSpec(forward.shape, lambda step, _: (0, 0)),
            ]
            + [pl.BlockSpec(memory_space=pl.ANY)] * aliased,
            out_specs=[
                pl.BlockSpec(whole, lambda step, _: (0, 0)),
                pl.BlockSpec((2, depths, size), lambda step, _: (0, 0, begin // rows)),
            ],
            scratch_shapes=[pltpu.VMEM((channels, 2 * wide), jnp.float32)] * (2 * groups)
            + [pltpu.VMEM((synth.shape[1], 2 * wide), jnp.bfloat16)] * groups
            + [pltpu.VMEM((4 * half, 2 * wide), jnp.bfloat16)] * groups
            + [pltpu.VMEM((synth.shape[0], 2 * wide), jnp.float32)] * groups
            + [pltpu.VMEM((4, half, wide), jnp.float32)] * groups
            + [pltpu.VMEM((groups, 16, wide), jnp.float32)],
        ),
        out_shape=[
            jax.ShapeDtypeStruct(whole, jnp.float32),
            jax.ShapeDtypeStruct((2, depths, pixels), jnp.float32),
        ],
        input_output_aliases={3 + chips: 1} if aliased else {},
        compiler_params=pltpu.CompilerParams(vmem_limit_bytes=VMEM),
        name="deconvolve",
    )(me, *cube, synth, forward, *([model] if aliased else []))
    return resid.reshape(2 * chips, group, rows, LANES), model


def chunk_spans(share):
    if share % 8 or share < 24:
        return ((0, share),)
    return ((0, 8), (8, 4), *((row, 8) for row in range(16, share, 8)), (12, 4))


def body(depths, *arrays):
    return run(depths, *arrays)


def run(depths, beam_images, beam_weights, offsets):
    beams, _, group, tile = beam_images.shape
    members = lax.axis_size("chan")
    sky = lax.axis_size("sky")
    pixels = tile // members
    lines = tile // LANES
    share = 2 * lines // members
    spans = chunk_spans(share)
    channels = group * members
    starts = offsets - lax.axis_index("sky") * tile
    images = beam_images.reshape(beams, 2, group, lines, LANES).transpose(0, 2, 3, 1, 4)
    images = images.reshape(beams, group, 2 * lines, LANES)
    weights = jnp.repeat(beam_weights.reshape(beams, lines, LANES), 2, axis=1)
    chips = members // 2
    me = lax.axis_index("chan").astype(jnp.int32)
    mine = me.reshape(1)
    ahead = [
        [(t * members + c, (t + 1) * members + (c ^ other)) for t in range(sky - 1) for c in range(members)]
        for other in range(2)
    ]
    backward_pairs = [(index + 1, index) for index in range(sky - 1)]
    both = ("sky", "chan")

    own, keep, give, weight = gather(chips, spans, starts, mine, weights, images)
    arrived = []
    for chunk in range(len(spans)):
        straight = lax.ppermute(keep[chunk], both, ahead[0])
        arrived.append((straight, lax.ppermute(give[chunk], both, ahead[1])))
    crossed = lax.ppermute(own[1], "chan", [(c, c ^ 1) for c in range(members)])
    arrived_w = lax.ppermute(weight[1], both, ahead[0])
    scale = (weight[0] + arrived_w + COMBINE_FLOOR).reshape(chips, 2, share, LANES)
    scale = lax.dynamic_index_in_dim(scale, lax.rem(me, 2), 1, keepdims=False)
    order = jnp.bitwise_xor(me, jnp.arange(members, dtype=jnp.int32))
    synth, forward = depth_tables(channels, depths, order)

    model = None
    resid, following = [], []
    for chunk, (begin, count) in enumerate(spans):
        cube = list(combine(begin, mine, scale, (own[0], crossed), arrived[chunk]))
        for index in range(1, chips):
            pairs = [(c, c ^ (2 * index)) for c in range(members)]
            cube[index] = lax.ppermute(cube[index], "chan", pairs)
        part, model = deconvolve(begin, depths, pixels, mine, cube, synth, forward, model)
        part = lax.all_to_all(part, "chan", 0, 0, tiled=True)
        resid.append(part)
        if chunk + 1 < len(spans):
            following.append(lax.ppermute(part, "sky", backward_pairs))
    parts = 2 if group % 2 == 0 else 1
    width = group // parts
    late = []
    for index in range(parts):
        late.append(lax.ppermute(part[:, index * width : (index + 1) * width], "sky", backward_pairs))
    outputs = None
    for index in range(parts):
        outputs = scatter(
            spans, index * width, width, starts, weights, resid, [*following, late[index]], outputs
        )
    outputs = outputs.reshape(beams, group, lines, 2, LANES).transpose(0, 3, 1, 2, 4)
    return outputs.reshape(beam_images.shape), model


DEPTHS = 512


def solution(mesh):
    in_specs = (P("sky", None, "chan", None), P("sky", None), P("sky"))
    out_specs = (P("sky", None, "chan", None), P(None, None, ("sky", "chan")))
    return jax.shard_map(
        functools.partial(body, DEPTHS),
        mesh=mesh,
        in_specs=in_specs,
        out_specs=out_specs,
        check_vma=False,
    )
```

```python
import functools

import jax
import jax.numpy as jnp
from jax import lax
from jax.experimental import pallas as pl
from jax.experimental.pallas import tpu as pltpu
from jax.sharding import PartitionSpec as P


ITERS = 3

BAND_LOW = 800000000.0
BAND_WIDTH = 288000000.0
LIGHT = 299792458.0
DEPTH_STEP = 20.0
COMBINE_FLOOR = 0.5
THRESH_FRAC = 0.25
THRESH_BASE = 0.005
STEP_GAIN = 0.5

LANES = 128
GROUP = 128
VMEM = 67043328


def split_rows(arrays):
    high = lax.reduce_precision(arrays, 8, 7)
    return high.astype(jnp.bfloat16), (arrays - high).astype(jnp.bfloat16)


def depth_tables(channels, depths, order):
    half = depths // 2
    channel = jnp.arange(channels, dtype=jnp.float32)
    freq = BAND_LOW + (channel + 0.5) * (BAND_WIDTH / channels)
    lam_sq = (LIGHT / freq) ** 2
    lam_sq = lam_sq - jnp.mean(lam_sq)
    lam_sq = lam_sq.reshape(order.shape[0], -1)[order].reshape(-1)
    depth = (jnp.arange(half, dtype=jnp.float32) + 1.0) * DEPTH_STEP
    angle = 2.0 * depth[:, None] * lam_sq[None, :]
    cosine = jnp.cos(angle)
    sine = jnp.sin(angle)
    ones = jnp.concatenate([jnp.ones((1, channels)), jnp.zeros((15, channels))], 0)
    synth = jnp.concatenate([cosine, sine, ones], 0) / channels * STEP_GAIN
    high, low = split_rows(synth)
    pad = -3 * channels % LANES
    synth = jnp.concatenate([high, high, low, jnp.zeros((high.shape[0], pad), jnp.bfloat16)], 1)
    forward = jnp.concatenate([cosine, sine], 0).T
    high, low = split_rows(forward)
    return synth, jnp.concatenate([high, high, low], 1)


def place(offsets_ref, beam):
    start = offsets_ref[beam]
    return lax.div(start, LANES), lax.rem(start, LANES)


def gather_kernel(spans, offsets_ref, me_ref, raw_ref, images_ref, *rest):
    chunks = len(spans)
    own, keep, give = rest[:2], rest[2 : 2 + chunks], rest[2 + chunks : 2 + 2 * chunks]
    wsum_refs, weights_ref = rest[2 + 2 * chunks : 4 + 2 * chunks], rest[4 + 2 * chunks]
    shifted = rest[5 + 2 * chunks :]
    first_core = lax.rem(me_ref[0], 2) == 0
    beams, block, rows, _ = images_ref.shape
    share = own[0].shape[2]
    step = max(64, 2 * share)
    lane = lax.broadcasted_iota(jnp.int32, (step, LANES), 1)
    places = [place(offsets_ref, beam) for beam in range(beams)]

    pixel = lane + LANES * (lax.broadcasted_iota(jnp.int32, (step, LANES), 0) // 2)

    def shift(scratch, beam, row, value):
        value = pltpu.roll(value, places[beam][1], 1)
        scratch[beam, row : row + step, :] = value
        scratch[beam, rows + row : rows + row + step, :] = value

    def total(scratch, row):
        inside = outside = 0.0
        for beam in range(beams):
            tile, rest_px = places[beam]
            base = rows + row - 2 * tile
            here = scratch[beam, pl.ds(base, step), :]
            before = scratch[beam, pl.ds(base - 2, step), :]
            part = jnp.where(lane >= rest_px, here, before)
            own_pixel = pixel >= offsets_ref[beam] - row // 2 * LANES
            inside = inside + jnp.where(own_pixel, part, 0.0)
            outside = outside + jnp.where(own_pixel, 0.0, part)
        return inside, outside

    @pl.when(pl.program_id(0) == 0)
    def _():
        for beam in range(beams):
            value = raw_ref[pl.ds(beam, rows // 2, stride=beams), :]
            for image in range(2):
                weights_ref[beam, pl.ds(image, rows // 2, stride=2), :] = value
        for beam in range(beams):
            for row in range(0, rows, step):
                shift(shifted[0], beam, row, weights_ref[beam, row : row + step, :])
        for row in range(0, rows, step):
            for wsum_ref, value in zip(wsum_refs, total(shifted[0], row)):
                wsum_ref[row : row + step, :] = value

    def emit(channel, row):
        inside, outside = total(shifted[channel], row)
        for index in range(0, step // share, 2):
            chip = (row // share + index) // 2
            cut = [slice(part * share, (part + 1) * share) for part in (index, index + 1)]
            for side, value in enumerate((inside, outside)):
                same = jnp.where(first_core, value[cut[0]], value[cut[1]])
                other = jnp.where(first_core, value[cut[1]], value[cut[0]])
                if side == 0:
                    own[0][chip, channel], own[1][chip, channel] = same, other
                    continue
                for part, (begin, count) in enumerate(spans):
                    keep[part][chip, channel] = same[begin : begin + count]
                    give[part][chip, channel] = other[begin : begin + count]

    for channel in range(block + 1):
        for row in range(0, rows, step):
            if channel < block:
                for beam in range(beams):
                    weight = weights_ref[beam, row : row + step, :]
                    value = images_ref[beam, channel, row : row + step, :]
                    shift(shifted[channel], beam, row, value * weight)
            if channel:
                emit(channel - 1, row)


def channel_block(channels):
    return max(size for size in range(1, 7) if channels % size == 0)


def gather(chips, spans, starts, me, weights, images):
    beams, channels, rows, _ = images.shape
    block = channel_block(channels)
    chunks = len(spans)
    counts = [rows // (2 * chips)] * 2 + [count for _, count in spans] * 2
    result = pl.pallas_call(
        functools.partial(gather_kernel, spans),
        grid_spec=pltpu.PrefetchScalarGridSpec(
            num_scalar_prefetch=2,
            grid=(channels // block,),
            in_specs=[
                pl.BlockSpec(weights.shape, lambda step, *_: (0, 0)),
                pl.BlockSpec((beams, block, rows, LANES), lambda step, *_: (0, step, 0, 0)),
            ],
            out_specs=[
                pl.BlockSpec((chips, block, count, LANES), lambda step, *_: (0, step, 0, 0))
                for count in counts
            ]
            + [pl.BlockSpec((rows, LANES), lambda step, *_: (0, 0))] * 2
            + [pl.BlockSpec((beams, rows, LANES), lambda step, *_: (0, 0, 0))],
            scratch_shapes=[pltpu.VMEM((beams, 2 * rows, LANES), jnp.float32)] * block,
        ),
        out_shape=[
            jax.ShapeDtypeStruct((chips, channels, count, LANES), jnp.float32) for count in counts
        ]
        + [jax.ShapeDtypeStruct((rows, LANES), jnp.float32)] * 2
        + [jax.ShapeDtypeStruct((beams, rows, LANES), jnp.float32)],
        compiler_params=pltpu.CompilerParams(vmem_limit_bytes=VMEM),
        name="gather",
    )(starts, me, weights, images)
    return result[:2], result[2 : 2 + chunks], result[2 + chunks : 2 + 2 * chunks], result[-3:]


def combine_kernel(first, me_ref, scale_ref, *refs):
    own, arrived, outs = refs[:2], refs[2:4], refs[4:]
    count = outs[0].shape[2]
    rows = slice(first, first + count)
    for index, out in enumerate(outs):
        chip = jnp.bitwise_xor(lax.div(me_ref[0], 2), index)
        scale = 1.0 / scale_ref[chip, rows, :]
        for side in range(2):
            total = own[side][chip, :, rows, :] + arrived[side][chip]
            out[side] = total * scale[None]


def combine(begin, me, scale, own, arrived):
    chips, channels, _, _ = own[0].shape
    count = arrived[0].shape[2]
    tall = max(8, count)
    block = channels // 3
    wide = pl.BlockSpec((chips, block, tall, LANES), lambda step, _: (0, step, begin // tall, 0))
    part = pl.BlockSpec((chips, block, count, LANES), lambda step, _: (0, step, 0, 0))
    return pl.pallas_call(
        functools.partial(combine_kernel, begin % tall),
        grid_spec=pltpu.PrefetchScalarGridSpec(
            num_scalar_prefetch=1,
            grid=(3,),
            in_specs=[pl.BlockSpec((chips, tall, LANES), lambda step, _: (0, begin // tall, 0))]
            + [wide] * 2
            + [part] * 2,
            out_specs=[pl.BlockSpec((2, block, count, LANES), lambda step, _: (0, step, 0, 0))]
            * chips,
        ),
        out_shape=[jax.ShapeDtypeStruct((2, channels, count, LANES), jnp.float32)] * chips,
        compiler_params=pltpu.CompilerParams(vmem_limit_bytes=VMEM),
        name="combine",
    )(me, scale, *own, *arrived)


def scatter_kernel(spans, aliased, offsets_ref, weights_ref, *rest):
    chunks = len(spans)
    if aliased:
        rest = rest[1:]
    own, following = rest[:chunks], rest[chunks : 2 * chunks]
    out_ref, joined = rest[2 * chunks], rest[2 * chunks + 1 :]
    beams, block, rows, _ = out_ref.shape
    members = own[0].shape[0]
    share = rows // members
    step = 64
    lane = lax.broadcasted_iota(jnp.int32, (step, LANES), 1)
    places = [place(offsets_ref, beam) for beam in range(beams)]
    for channel in range(block):
        for half, pieces in enumerate((own, following)):
            for member in range(members):
                for piece, (begin, count) in zip(pieces, spans):
                    row = half * rows + member * share + begin
                    joined[channel][row : row + count, :] = piece[member, channel]
        for beam in range(beams):
            tile, rest_px = places[beam]
            for row in range(0, rows, step):
                base = 2 * tile + row
                here = joined[channel][pl.ds(base, step), :]
                after = joined[channel][pl.ds(base + 2, step), :]
                value = jnp.where(lane >= rest_px, here, after)
                value = pltpu.roll(value, lax.rem(LANES - rest_px, LANES), 1)
                out_ref[beam, channel, row : row + step, :] = (
                    value * weights_ref[beam, row : row + step, :]
                )


def scatter(spans, first, width, starts, weights, own, following, output):
    beams, rows, _ = weights.shape
    members, channels, _, _ = own[0].shape
    block = max(size for size in range(1, 10) if width % size == 0)
    aliased = output is not None

    def piece(array, count):
        base = first // block if array.shape[1] == channels else 0
        shape = (members, block, count, LANES)
        return pl.BlockSpec(shape, lambda step, _: (0, base + step, 0, 0))

    return pl.pallas_call(
        functools.partial(scatter_kernel, spans, aliased),
        grid_spec=pltpu.PrefetchScalarGridSpec(
            num_scalar_prefetch=1,
            grid=(width // block,),
            in_specs=[pl.BlockSpec((beams, rows, LANES), lambda step, _: (0, 0, 0))]
            + [pl.BlockSpec(memory_space=pl.ANY)] * aliased
            + [piece(array, count) for part in (own, following) for array, (_, count) in zip(part, spans)],
            out_specs=pl.BlockSpec(
                (beams, block, rows, LANES), lambda step, _: (0, first // block + step, 0, 0)
            ),
            scratch_shapes=[pltpu.VMEM((2 * rows, LANES), jnp.float32)] * block,
        ),
        out_shape=jax.ShapeDtypeStruct((beams, channels, rows, LANES), jnp.float32),
        input_output_aliases={2: 0} if aliased else {},
        compiler_params=pltpu.CompilerParams(vmem_limit_bytes=VMEM),
        name="scatter",
    )(starts, weights, *([output] if aliased else []), *own, *following)


def split(value):
    high = value.astype(jnp.bfloat16)
    return high, (value - high.astype(jnp.float32)).astype(jnp.bfloat16)


def deconvolve_kernel(aliased, groups, chips, me_ref, *refs):
    flat_refs, refs = refs[:chips], refs[chips:]
    if aliased:
        refs = refs[:2] + refs[3:]
    synth_ref, forward_ref, resid_ref, model_ref = refs[:4]
    refs = (None, *refs)
    flat, resid, x, y, product, field = (
        refs[5 + kind * groups : 5 + (kind + 1) * groups] for kind in range(6)
    )
    level = refs[5 + 6 * groups]
    channels = flat[0].shape[0]
    half = field[0].shape[1]
    pixels = field[0].shape[2]
    tiles = pixels // LANES
    stride = 2 * groups * tiles
    sub = 16
    left, right = slice(0, pixels), slice(pixels, 2 * pixels)
    last = lax.broadcasted_iota(jnp.int32, (sub, pixels), 0) == sub - 1

    places = [
        (tile, q, slice(q * pixels + tile * LANES, q * pixels + (tile + 1) * LANES))
        for tile in range(tiles)
        for q in range(2)
    ]

    def feed(group, row, value):
        high, low = split(value)
        for part, piece in enumerate((high, low, high)):
            x[group][part * channels + row : part * channels + row + sub, :] = piece

    def load(group):
        for tile, q, lanes in places:
            size = channels // chips
            for chip, ref in enumerate(flat_refs):
                flat[group][chip * size : (chip + 1) * size, lanes] = ref[
                    pl.ds(2 * (group * tiles + tile) + q, size, stride=stride), :
                ]
        for row in range(0, channels, sub):
            feed(group, row, flat[group][row : row + sub, :])
        extra = x[group].shape[0] - 3 * channels
        x[group][3 * channels :, :] = jnp.zeros((extra, 2 * pixels), jnp.bfloat16)

    def synthesize(group):
        product[group][...] = jnp.dot(
            synth_ref[...], x[group][...], preferred_element_type=jnp.float32
        )

    def project(group):
        resid[group][...] = jnp.dot(
            forward_ref[:, : 4 * half], y[group][...], preferred_element_type=jnp.float32
        ) + jnp.dot(
            forward_ref[:, 4 * half :], y[group][: 2 * half, :], preferred_element_type=jnp.float32
        )

    def step_of(group, row, old):
        rows, low_rows = slice(row, row + sub), slice(half + row, half + row + sub)
        cos_q, cos_u = product[group][rows, left], product[group][rows, right]
        sin_q, sin_u = product[group][low_rows, left], product[group][low_rows, right]
        real_p, real_n = cos_q + sin_u, cos_q - sin_u
        imag_p, imag_n = cos_u - sin_q, cos_u + sin_q
        if row + sub == half:
            real_p = jnp.where(last, product[group][2 * half : 2 * half + 1, left], real_p)
            imag_p = jnp.where(last, product[group][2 * half : 2 * half + 1, right], imag_p)
        values = [real_p, real_n, imag_p, imag_n]
        if old:
            values = [value + field[group][part, rows, :] for part, value in enumerate(values)]
        real_p, real_n, imag_p, imag_n = values
        return values, real_p * real_p + imag_p * imag_p, real_n * real_n + imag_n * imag_n

    def shrink(group, old):
        if not old:
            largest = jnp.zeros((sub, pixels), jnp.float32)
            for row in range(0, half, sub):
                _, power_p, power_n = step_of(group, row, old)
                largest = jnp.maximum(largest, jnp.maximum(power_p, power_n))
            top = jnp.sqrt(jnp.max(largest, axis=0, keepdims=True))
            level[group] = jnp.broadcast_to(
                THRESH_FRAC / STEP_GAIN * top + THRESH_BASE, level.shape[1:]
            )
        limit = level[group]
        for row in range(0, half, sub):
            rows = slice(row, row + sub)
            values, power_p, power_n = step_of(group, row, old)
            factor_p = jnp.maximum(1.0 - limit * lax.rsqrt(power_p), 0.0)
            factor_n = jnp.maximum(1.0 - limit * lax.rsqrt(power_n), 0.0)
            values = [
                value * factor for value, factor in zip(values, (factor_p, factor_n) * 2)
            ]
            for part, value in enumerate(values):
                field[group][part, rows, :] = value
            real_p, real_n, imag_p, imag_n = values
            if row + sub == half:
                real_p, imag_p = jnp.where(last, 0.0, real_p), jnp.where(last, 0.0, imag_p)
            for base, lanes, value in (
                (0, left, real_p + real_n),
                (0, right, imag_p + imag_n),
                (half, left, imag_n - imag_p),
                (half, right, real_p - real_n),
            ):
                high, low = split(value)
                y[group][base + row : base + row + sub, lanes] = high
                y[group][2 * half + base + row : 2 * half + base + row + sub, lanes] = low

    def subtract(group):
        middle = jnp.concatenate(
            [field[group][0, half - 1 : half, :], field[group][2, half - 1 : half, :]], 1
        )
        for row in range(0, channels, sub):
            rows = slice(row, row + sub)
            value = flat[group][rows, :] - (resid[group][rows, :] + middle)
            resid[group][rows, :] = value
            feed(group, row, value)

    def iterate(old):
        for group in range(groups):
            shrink(group, old)
            if group + 1 < groups:
                synthesize(group + 1)
            else:
                project(0)
        for group in range(groups):
            subtract(group)
            if group + 1 < groups:
                project(group + 1)
            else:
                synthesize(0)

    for group in range(groups):
        load(group)
    synthesize(0)
    iterate(False)

    def repeat(number, carry):
        iterate(True)
        return carry

    lax.fori_loop(1, ITERS, repeat, 0)

    for group in range(groups):
        for tile, q, side in places:
            size = channels // (2 * chips)
            for part in range(2 * chips):
                base = jnp.bitwise_xor(me_ref[0], part) * (size * stride)
                base = base + (2 * (group * tiles + tile) + q)
                resid_ref[pl.ds(base, size, stride=stride), :] = resid[group][
                    part * size : (part + 1) * size, side
                ]
        lanes = slice(group * pixels, (group + 1) * pixels)
        for part in range(2):
            model_ref[part, half : half + 1, lanes] = field[group][2 * part, half - 1 : half, :]
            model_ref[part, half + 1 :, lanes] = field[group][2 * part, : half - 1, :]

    turn = 32

    def reverse(index, carry):
        row = pl.multiple_of(index * turn, turn)
        for part in range(2):
            value = jnp.concatenate(
                [field[group][2 * part + 1, pl.ds(row, turn), :] for group in range(groups)], 1
            )
            for line in range(turn):
                model_ref[part, pl.ds(half - 1 - line - row, 1), :] = value[line : line + 1, :]
        return carry

    lax.fori_loop(0, half // turn, reverse, 0)


def deconvolve(begin, depths, pixels, me, cube, synth, forward, model):
    chips = len(cube)
    _, group, rows, _ = cube[0].shape
    channels = 2 * chips * group
    half = depths // 2
    size = rows // 2 * LANES
    groups = max(1, size // GROUP)
    wide = size // groups
    cube = [part.reshape(-1, LANES) for part in cube]
    whole = (channels * rows, LANES)
    aliased = model is not None
    resid, model = pl.pallas_call(
        functools.partial(deconvolve_kernel, aliased, groups, chips),
        grid_spec=pltpu.PrefetchScalarGridSpec(
            num_scalar_prefetch=1,
            grid=(1,),
            in_specs=[pl.BlockSpec(part.shape, lambda step, _: (0, 0)) for part in cube]
            + [
                pl.BlockSpec(synth.shape, lambda step, _: (0, 0)),
                pl.BlockSpec(forward.shape, lambda step, _: (0, 0)),
            ]
            + [pl.BlockSpec(memory_space=pl.ANY)] * aliased,
            out_specs=[
                pl.BlockSpec(whole, lambda step, _: (0, 0)),
                pl.BlockSpec((2, depths, size), lambda step, _: (0, 0, begin // rows)),
            ],
            scratch_shapes=[pltpu.VMEM((channels, 2 * wide), jnp.float32)] * (2 * groups)
            + [pltpu.VMEM((synth.shape[1], 2 * wide), jnp.bfloat16)] * groups
            + [pltpu.VMEM((4 * half, 2 * wide), jnp.bfloat16)] * groups
            + [pltpu.VMEM((synth.shape[0], 2 * wide), jnp.float32)] * groups
            + [pltpu.VMEM((4, half, wide), jnp.float32)] * groups
            + [pltpu.VMEM((groups, 16, wide), jnp.float32)],
        ),
        out_shape=[
            jax.ShapeDtypeStruct(whole, jnp.float32),
            jax.ShapeDtypeStruct((2, depths, pixels), jnp.float32),
        ],
        input_output_aliases={3 + chips: 1} if aliased else {},
        compiler_params=pltpu.CompilerParams(vmem_limit_bytes=VMEM),
        name="deconvolve",
    )(me, *cube, synth, forward, *([model] if aliased else []))
    return resid.reshape(2 * chips, group, rows, LANES), model


def chunk_spans(share):
    if share % 8:
        return ((0, share),)
    return tuple((row, 8) for row in range(0, share, 8))


def body(depths, *arrays):
    return run(depths, *arrays)


def run(depths, beam_images, beam_weights, offsets):
    beams, _, group, tile = beam_images.shape
    members = lax.axis_size("chan")
    sky = lax.axis_size("sky")
    pixels = tile // members
    lines = tile // LANES
    share = 2 * lines // members
    spans = chunk_spans(share)
    channels = group * members
    starts = offsets - lax.axis_index("sky") * tile
    images = beam_images.reshape(beams, 2, group, lines, LANES).transpose(0, 2, 3, 1, 4)
    images = images.reshape(beams, group, 2 * lines, LANES)
    weights = beam_weights.reshape(beams, lines, LANES).transpose(1, 0, 2).reshape(-1, LANES)
    chips = members // 2
    me = lax.axis_index("chan").astype(jnp.int32)
    mine = me.reshape(1)
    ahead = [
        [(t * members + c, (t + 1) * members + (c ^ other)) for t in range(sky - 1) for c in range(members)]
        for other in range(2)
    ]
    backward_pairs = [(index + 1, index) for index in range(sky - 1)]
    both = ("sky", "chan")

    own, keep, give, (*weight, weights) = gather(chips, spans, starts, mine, weights, images)
    arrived = []
    for chunk in range(len(spans)):
        straight = lax.ppermute(keep[chunk], both, ahead[0])
        arrived.append((straight, lax.ppermute(give[chunk], both, ahead[1])))
    crossed = lax.ppermute(own[1], "chan", [(c, c ^ 1) for c in range(members)])
    arrived_w = lax.ppermute(weight[1], both, ahead[0])
    scale = (weight[0] + arrived_w + COMBINE_FLOOR).reshape(chips, 2, share, LANES)
    scale = lax.dynamic_index_in_dim(scale, lax.rem(me, 2), 1, keepdims=False)
    order = jnp.bitwise_xor(me, jnp.arange(members, dtype=jnp.int32))
    synth, forward = depth_tables(channels, depths, order)

    model = None
    resid, following = [], []
    for chunk, (begin, count) in enumerate(spans):
        cube = list(combine(begin, mine, scale, (own[0], crossed), arrived[chunk]))
        for index in range(1, chips):
            pairs = [(c, c ^ (2 * index)) for c in range(members)]
            cube[index] = lax.ppermute(cube[index], "chan", pairs)
        part, model = deconvolve(begin, depths, pixels, mine, cube, synth, forward, model)
        part = lax.all_to_all(part, "chan", 0, 0, tiled=True)
        resid.append(part)
        if chunk + 1 < len(spans):
            following.append(lax.ppermute(part, "sky", backward_pairs))
    parts = 2 if group % 2 == 0 else 1
    width = group // parts
    late = []
    for index in range(parts):
        late.append(lax.ppermute(part[:, index * width : (index + 1) * width], "sky", backward_pairs))
    outputs = None
    for index in range(parts):
        outputs = scatter(
            spans, index * width, width, starts, weights, resid, [*following, late[index]], outputs
        )
    outputs = outputs.reshape(beams, group, lines, 2, LANES).transpose(0, 3, 1, 2, 4)
    return outputs.reshape(beam_images.shape), model


DEPTHS = 512


def solution(mesh):
    in_specs = (P("sky", None, "chan", None), P("sky", None), P("sky"))
    out_specs = (P("sky", None, "chan", None), P(None, None, ("sky", "chan")))
    return jax.shard_map(
        functools.partial(body, DEPTHS),
        mesh=mesh,
        in_specs=in_specs,
        out_specs=out_specs,
        check_vma=False,
    )
```
